256 devices in a mesh: ctx: 32 (over z, y), head: 8 (over x, core).
Axes of the slice: x: 4, y: 4, z: 8, core: 2. Of those that a mesh axis runs over, the one named last changes fastest.
Arguments:
- queries: bfloat16 [4096, 8192], P('ctx', 'head'), may hold values from -6 to 6
- key_rows: bfloat16 [4096, 1024], P(('ctx', 'head')), may hold values from -6 to 6
- value_matrix_rows: bfloat16 [4096, 1024], P(('ctx', 'head')), may hold values from -6 to 6
- grad_out: bfloat16 [4096, 8192], P('ctx', 'head'), may hold values from -6 to 6
- doc_ids: int32 [4096], replicated, may hold values from 0 to 3, never falling along the last dimension, each value on 1 to 2048 neighbouring positions
- block_owner: int32 [32, 32], replicated, may hold values from 0 to 31, each once within a row
Outputs:
- attention: bfloat16 [4096, 8192], P('ctx', 'head')
- owned_lse: float32 [64, 4096], P('head', 'ctx')
- grad_query: bfloat16 [4096, 8192], P('ctx', 'head')
- key_gradient: bfloat16 [4096, 1024], P(('ctx', 'head'))
- value_gradient: bfloat16 [4096, 1024], P(('ctx', 'head'))
The draws below stay inside these ranges and needn't reach their ends.
Inputs may be any that keep to these rules, and one draw needn't show every extreme that they name: `doc_ids`: never falls along the tokens; every document holds 1 to 2048 tokens. `block_owner`: entry [d, i] names the device that owns block i (tokens d * 128 + i * 4 onward, 4 of them) of token shard d; each row names every device once.
All inputs are finite; a program needn't handle non-finite values.
Results may differ from the reference program's by a relative error of at most 0.02.
Values may be sent and summed in bfloat16 or wider, within the bound.
A program may use at most 64 MiB of HBM per device.

```python
import math
import jax
import jax.numpy as jnp
import numpy as np
from jax import lax

HQ = 64
KEY_VALUE_HEADS = 8
HEAD_SIZE = 128
DOCS = 4
QUERY_PER_KV = 8
SHARDS = 32
PACKED_TOKENS = 4096
BLK = 4
MOST_DOC = 2048


def draw_queries(key, part):
    sampled_plan = jax.random.normal(jax.random.fold_in(key, 1), (PACKED_TOKENS, HQ * HEAD_SIZE), jnp.float32)
    return jnp.clip(sampled_plan, -6.0, 6.0).astype(jnp.bfloat16)


def draw_key_rows(key, part):
    sampled_plan = jax.random.normal(jax.random.fold_in(key, 3), (PACKED_TOKENS, KEY_VALUE_HEADS * HEAD_SIZE), jnp.float32)
    return jnp.clip(sampled_plan, -6.0, 6.0).astype(jnp.bfloat16)


def steps_of(stream_key, extent, pieces, low, high):
    level = 1.0
    for position, shards_of in pieces:
        heights = jax.random.uniform(jax.random.fold_in(jax.random.fold_in(stream_key, 6), position), (shards_of,), jnp.float32, low / len(pieces), high / len(pieces))
        level = level * jnp.repeat(jnp.exp(heights), extent[position] // shards_of).reshape((-1,) + (1,) * (len(extent) - 1 - position))
    return level


def profile(amount, total, most, skew):
    loads = [(1 << 20) // math.isqrt(grade ** skew) + 1 for grade in range(2, amount + 1)]
    spare, counts = total - most - (amount - 1), [1] * (amount - 1)
    while spare > 0:
        candidates = [i for i in range(amount - 1) if counts[i] < most]
        mass, remaining = sum([loads[i] for i in candidates]), spare
        for i in candidates:
            extra = min(most - counts[i], max(1, remaining * loads[i] // mass), spare)
            counts[i] = counts[i] + extra
            spare = spare - extra
    return np.array([most] + counts)


def uneven(stream_key, count, total, reach, skew):
    if count == 2:
        one = jax.random.randint(stream_key, (), max(1, total - reach), min(reach, total - 1) + 1)
        return jnp.stack([one, total - one])
    sizes = jnp.asarray(profile(count, total, reach, skew), jnp.int32)
    twos = (count - 1) // 2
    donor, sink = sizes[1:1 + 2 * twos:2], sizes[2:2 + 2 * twos:2]
    room = jnp.minimum(donor - 1, reach - sink)
    passed = jax.random.randint(jax.random.fold_in(stream_key, 1), (twos,), 0, 1 << 20) % (room + 1)
    sizes = sizes.at[1:1 + 2 * twos:2].set(donor - passed).at[2:2 + 2 * twos:2].set(sink + passed)
    return sizes[jax.random.permutation(jax.random.fold_in(stream_key, 2), count)]


def centred(own_key, dims, spread, reach, pieces=(), held_as=jnp.bfloat16):
    result = spread * jax.random.normal(own_key, dims, jnp.float32)
    if pieces:
        result = result * steps_of(own_key, dims, pieces, -0.22, 0.18)
    return jnp.clip(result, -reach, reach).astype(held_as)


def setup_inputs(seed: int = 0) -> dict:
    key_list = jax.random.split(jax.random.key(seed), 7)
    return {
        "queries": draw_queries(jax.random.fold_in(key_list[6], 71), 0),
        "key_rows": draw_key_rows(jax.random.fold_in(key_list[6], 71), 0),
        "value_matrix_rows": centred(key_list[2], (PACKED_TOKENS, KEY_VALUE_HEADS * HEAD_SIZE), 1.0, 6.0, ((0, 256),)),
        "grad_out": centred(key_list[3], (PACKED_TOKENS, HQ * HEAD_SIZE), 1.0, 6.0, ((0, 32), (1, 8))),
        "doc_ids": jnp.searchsorted(jnp.cumsum(uneven(key_list[4], DOCS, PACKED_TOKENS, MOST_DOC, 2)), jnp.arange(PACKED_TOKENS), side="right").astype(jnp.int32),
        "block_owner": jax.vmap(lambda own: jax.random.permutation(own, SHARDS))(jax.random.split(key_list[5], SHARDS)).reshape((SHARDS, SHARDS)).astype(jnp.int32),
    }


mask_value = -1.0e30


def reference(queries, key_rows, value_matrix_rows, grad_out, doc_ids, block_owner):
    score_scale = HEAD_SIZE ** -0.5
    positions = jnp.arange(PACKED_TOKENS, dtype=jnp.int32)
    allowed = (doc_ids[:, None] == doc_ids[None, :]) & (positions[None, :] <= positions[:, None])

    def per_head(head_index):
        group_index = head_index // QUERY_PER_KV
        query_head = lax.dynamic_slice_in_dim(queries, (head_index * HEAD_SIZE).astype(jnp.int32), HEAD_SIZE, 1)
        grad_head = lax.dynamic_slice_in_dim(grad_out, (head_index * HEAD_SIZE).astype(jnp.int32), HEAD_SIZE, 1)
        key_head = lax.dynamic_slice_in_dim(key_rows, (group_index * HEAD_SIZE).astype(jnp.int32), HEAD_SIZE, 1)
        value_head = lax.dynamic_slice_in_dim(value_matrix_rows, (group_index * HEAD_SIZE).astype(jnp.int32), HEAD_SIZE, 1)
        scores = jnp.dot(query_head, key_head.T, preferred_element_type=jnp.float32) * score_scale
        masked = jnp.where(allowed, scores, mask_value)
        row_max = jnp.max(masked, axis=1)
        weights_raw = jnp.where(allowed, jnp.exp(masked - row_max[:, None]), 0.0)
        row_sum = jnp.sum(weights_raw, axis=1)
        output_head = (jnp.dot(weights_raw.astype(jnp.bfloat16), value_head, preferred_element_type=jnp.float32) / row_sum[:, None]).astype(jnp.bfloat16)
        log_norm = row_max + jnp.log(row_sum)
        row_delta = jnp.sum(grad_head.astype(jnp.float32) * output_head.astype(jnp.float32), axis=1)
        probability = jnp.where(allowed, jnp.exp(masked - log_norm[:, None]), 0.0)
        dprob = jnp.dot(grad_head, value_head.T, preferred_element_type=jnp.float32)
        dscore = probability * (dprob - row_delta[:, None])
        dscore_low = dscore.astype(jnp.bfloat16)
        query_grad = (jnp.dot(dscore_low, key_head, preferred_element_type=jnp.float32) * score_scale).astype(jnp.bfloat16)
        key_grad = jnp.dot(dscore_low.T, query_head, preferred_element_type=jnp.float32) * score_scale
        value_grad = jnp.dot(probability.astype(jnp.bfloat16).T, grad_head, preferred_element_type=jnp.float32)
        return output_head, log_norm, query_grad, key_grad, value_grad

    result_list = lax.map(per_head, jnp.arange(HQ, dtype=jnp.int32))
    attention = result_list[0].transpose(1, 0, 2).reshape(PACKED_TOKENS, HQ * HEAD_SIZE)
    log_norm = result_list[1]
    grad_query = result_list[2].transpose(1, 0, 2).reshape(PACKED_TOKENS, HQ * HEAD_SIZE)
    key_gradient = result_list[3].reshape(KEY_VALUE_HEADS, QUERY_PER_KV, PACKED_TOKENS, HEAD_SIZE).sum(axis=1).transpose(1, 0, 2).reshape(PACKED_TOKENS, KEY_VALUE_HEADS * HEAD_SIZE).astype(jnp.bfloat16)
    value_gradient = result_list[4].reshape(KEY_VALUE_HEADS, QUERY_PER_KV, PACKED_TOKENS, HEAD_SIZE).sum(axis=1).transpose(1, 0, 2).reshape(PACKED_TOKENS, KEY_VALUE_HEADS * HEAD_SIZE).astype(jnp.bfloat16)
    inverse = jnp.argsort(block_owner, axis=1).astype(jnp.int32)
    split_lse = log_norm.reshape(HQ, SHARDS, SHARDS, BLK)
    gather_index = jnp.broadcast_to(inverse[None, :, :, None], split_lse.shape)
    picked = jnp.take_along_axis(split_lse, gather_index, axis=2)
    owned_lse = picked.transpose(0, 2, 1, 3).reshape(HQ, PACKED_TOKENS)
    return attention, owned_lse, grad_query, key_gradient, value_gradient
```

```python
import jax
import jax.numpy as jnp
from jax import lax
from jax.experimental import pallas as pl
from jax.experimental.pallas import tpu as pltpu
from jax.sharding import PartitionSpec as P

D = 128
TOK = 128
HG = 8
ROWS = HG * TOK
CHUNK = 256
NCHUNK = ROWS // CHUNK
NZ, NY = 8, 4
NH = 8
TOKDEV = 16
OWN = 16
LOG2E = 1.4426950408889634
LN2 = 0.6931471805599453
NEG = -1e30
SCALE = D**-0.5
F32 = jnp.float32
BF16 = jnp.bfloat16
MESH = pl.DeviceIdType.MESH


def dot(a, b):
    return jnp.dot(a, b, preferred_element_type=F32)


def kernel(
    q_hbm, k_ref, v_ref, g_hbm, doc_ref, owner_ref,
    att_ref, lse_ref, gq_ref, gk_ref, gv_ref,
    q_in, g_in, qt, gt, qs, gs, kv, stage, pbuf, dsb, plb, tr, ot, dqt, mrun, lrun, mgrp, delta,
    part, yrecv, zrecv, zsend, total, hrecv, lown, lgat,
    load_sem, ha_send, ha_recv, kz_send, ky_send, kv_recv,
    gy_send, gy_recv, gz_send, gz_recv, hb_send, hb_recv, ly_send, ly_recv, lz_send, lz_recv,
):
    ctx = lax.axis_index("ctx")
    head = lax.axis_index("head")
    z = ctx // NY
    y = ctx % NY

    load_q = pltpu.make_async_copy(q_hbm, q_in, load_sem.at[0])
    load_g = pltpu.make_async_copy(g_hbm, g_in, load_sem.at[1])
    load_q.start()
    load_g.start()

    def at_head(i):
        return (ctx, (head + i) % NH)

    def at_y(i):
        return (z * NY + (y + i) % NY, head)

    def at_z(i):
        return (((z + i) % NZ) * NY + y, head)

    barrier = pltpu.get_barrier_semaphore()
    for i in range(1, NH):
        pl.semaphore_signal(barrier, inc=1, device_id=at_head(i), device_id_type=MESH)
    for i in range(1, NY):
        pl.semaphore_signal(barrier, inc=1, device_id=at_y(i), device_id_type=MESH)
    for i in range(1, NZ):
        pl.semaphore_signal(barrier, inc=1, device_id=at_z(i), device_id_type=MESH)

    for h in range(NH):
        stage[h, 0] = k_ref[:, h * D : (h + 1) * D]
        stage[h, 1] = v_ref[:, h * D : (h + 1) * D]
    pl.semaphore_wait(barrier, NH + NY + NZ - 3)

    def remote(src, dst, ssem, rsem, to):
        return pltpu.make_async_remote_copy(
            src_ref=src, dst_ref=dst, send_sem=ssem, recv_sem=rsem, device_id=to, device_id_type=MESH
        )

    def head_copy(i):
        to = (head + i) % NH
        rows = pl.ds(pl.multiple_of(head * TOKDEV, TOKDEV), TOKDEV)
        return remote(
            stage.at[to], kv.at[OWN, :, rows, :], ha_send.at[i], ha_recv.at[i], at_head(i)
        )

    def head_arrival(i):
        rows = pl.ds(pl.multiple_of(((head + NH - i) % NH) * TOKDEV, TOKDEV), TOKDEV)
        return remote(stage.at[0], kv.at[OWN, :, rows, :], ha_send.at[i], ha_recv.at[i], at_head(i))

    for i in range(1, NH):
        head_copy(i).start()
    kv[OWN, :, pl.ds(pl.multiple_of(head * TOKDEV, TOKDEV), TOKDEV), :] = stage[head]

    load_q.wait()
    load_g.wait()
    for h in range(HG):
        cols = slice(h * D, (h + 1) * D)
        qh, gh = q_in[:, cols], g_in[:, cols]
        qs[cols, :] = qh
        gs[cols, :] = gh
        qt[:, cols] = qh.T
        gt[:, cols] = gh.T

    @pl.when(z < 4)
    def _():
        for j in range(NY):

            @pl.when(y <= j)
            def _(j=j):
                kv[12 + j] = jnp.zeros((2, TOK, D), BF16)

    for i in range(1, NH):
        head_arrival(i).wait_recv()

    def chain_copy(hop):
        src = kv.at[OWN] if hop == 1 else kv.at[4 * (hop - 2) + y]
        dst = kv.at[4 * (hop - 1) + y]
        to = (jnp.minimum(z + 1, NZ - 1) * NY + y, head)
        return remote(src, dst, kz_send.at[hop - 1], kv_recv.at[4 * (hop - 1) + y], to)

    def chain_goes(hop):
        return (z < NZ - 1) & (z >= hop - 1)

    def chain_start(hop):
        @pl.when(chain_goes(hop))
        def _():
            chain_copy(hop).start()

    def spread_copy(level, i):
        src = kv.at[OWN] if level == 0 else kv.at[4 * (level - 1) + y]
        slot = 12 + y if level in (0, 4) else 4 * (level - 1) + y
        return remote(src, kv.at[slot], ky_send.at[3 * level + i - 1], kv_recv.at[slot], at_y(i))

    def spread_goes(level, i):
        if level == 0:
            return (y + i) < NY
        if level == 4:
            return (z >= 4) & ((y + i) >= NY)
        return z >= level

    def spread_start(level):
        for i in range(1, NY):

            @pl.when(spread_goes(level, i))
            def _(i=i):
                spread_copy(level, i).start()

    def slot_arrival(slot):
        remote(kv.at[slot], kv.at[slot], kz_send.at[0], kv_recv.at[slot], at_y(1)).wait_recv()

    chain_start(1)
    spread_start(0)

    docs = doc_ref[...]
    mine = doc_ref[pl.ds(ctx, 1), :]
    starts = jnp.zeros((1, TOK), F32)
    for v in range(1, 4):
        below = jnp.where(docs < v, 1.0, 0.0).astype(F32)
        count = jnp.sum(jnp.sum(below, axis=0, keepdims=True), axis=1, keepdims=True)
        starts = jnp.where(mine == v, count, starts)
    starts = jnp.concatenate([starts, starts], axis=1)
    tpos = lax.broadcasted_iota(jnp.int32, (1, TOK), 1).astype(F32)
    tpos = jnp.concatenate([tpos, tpos], axis=1) + (ctx * TOK).astype(F32)

    def positions(bases):
        step = lax.broadcasted_iota(jnp.int32, (TOK, 1), 0).astype(F32)
        return jnp.concatenate([step + b.astype(F32) for b in bases], axis=0)

    def chunk_of(c):
        return pl.ds(pl.multiple_of(c * CHUNK, CHUNK), CHUNK)

    def forward(group, slot0, count, bases, diagonal):
        n = count * TOK
        keys = kv[slot0 : slot0 + count, 0].reshape(n, D)
        tr[:, :n] = kv[slot0 : slot0 + count, 1].reshape(n, D).T
        kpos = positions(bases)

        def step(c, carry):
            cols = chunk_of(c)
            s = dot(keys, qt[:, cols]) * (SCALE * LOG2E)
            allowed = kpos >= starts
            if diagonal:
                allowed = allowed & (kpos <= tpos)
            s = jnp.where(allowed, s, NEG)
            top = jnp.max(s, axis=0, keepdims=True)
            if not diagonal:
                before = mrun[:, cols]
                top = jnp.maximum(before, top)
                fade = jnp.exp2(before - top)
            p = jnp.exp2(s - top)
            mass = jnp.sum(p, axis=0, keepdims=True)
            low = p.astype(BF16)
            pbuf[slot0 * TOK : slot0 * TOK + n, cols] = low
            part_o = dot(tr[:, :n], low)
            if diagonal:
                lrun[:, cols] = mass
                ot[:, cols] = part_o
            else:
                lrun[:, cols] = lrun[:, cols] * fade + mass
                ot[:, cols] = ot[:, cols] * fade + part_o
            mrun[:, cols] = top
            mgrp[group : group + 1, cols] = top
            return carry

        lax.fori_loop(0, NCHUNK, step, 0)

    def level_bases(level):
        return [((z - level) * NY + j) * TOK for j in range(NY)]

    mix_bases = [jnp.where(j < y, z * NY + j, (z - 4) * NY + j) * TOK for j in range(NY)]

    def pass_on(level):
        @pl.when(z >= level)
        def _():
            slot_arrival(4 * (level - 1) + y)

        if level < 4:
            chain_start(level + 1)
        spread_start(level)

    def await_level(level):
        @pl.when(z >= level)
        def _():
            for i in range(1, NY):
                slot_arrival(4 * (level - 1) + (y + i) % NY)

    forward(0, OWN, 1, [ctx * TOK], True)
    pass_on(1)
    pass_on(2)
    for level in (1, 2, 3):
        await_level(level)

        @pl.when(z >= level)
        def _(level=level):
            forward(level, 4 * (level - 1), 4, level_bases(level), False)

        if level < 3:
            pass_on(level + 2)
    for i in range(1, NY):
        other = (y + i) % NY

        @pl.when((other < y) | (z >= 4))
        def _(other=other):
            slot_arrival(12 + other)

    forward(4, 12, 4, mix_bases, False)

    def finish(c, carry):
        cols = chunk_of(c)
        mass = lrun[:, cols]
        out = (ot[:, cols] / mass).astype(BF16)
        wide = out.astype(F32)
        ot[:, cols] = wide
        delta[:, cols] = jnp.sum(gt[:, cols].astype(F32) * wide, axis=0, keepdims=True)
        return carry

    lax.fori_loop(0, NCHUNK, finish, 0)
    norm = mrun[...] * LN2 + jnp.log(lrun[...])
    for h in range(HG):
        cols = slice(h * D, (h + 1) * D)
        lown[h : h + 1, :] = norm[:, cols]
    reps = lax.broadcasted_iota(jnp.int32, (32, TOK), 1) // 4 == lax.broadcasted_iota(
        jnp.int32, (32, TOK), 0
    )
    owners = dot(owner_ref[pl.ds(ctx, 1), :].astype(F32), jnp.where(reps, 1.0, 0.0).astype(F32))
    to_col = lax.broadcasted_iota(jnp.int32, (TOK, TOK), 0)
    from_tok = lax.broadcasted_iota(jnp.int32, (TOK, TOK), 1)
    hit = (owners == (to_col // 4).astype(F32)) & (to_col % 4 == from_tok % 4)
    lgat[z, y] = lax.dot_general(
        lown[...],
        jnp.where(hit, 1.0, 0.0).astype(F32),
        (((1,), (1,)), ((), ())),
        precision=lax.Precision.HIGHEST,
        preferred_element_type=F32,
    )

    def lse_y(i):
        return remote(lgat.at[z, y], lgat.at[z, y], ly_send.at[i], ly_recv.at[i], at_y(i))

    def lse_y_arrival(i):
        other = (y + NY - i) % NY
        return remote(lgat.at[z, other], lgat.at[z, other], ly_send.at[i], ly_recv.at[i], at_y(i))

    def lse_z(i):
        return remote(lgat.at[z], lgat.at[z], lz_send.at[i], lz_recv.at[i], at_z(i))

    def lse_z_arrival(i):
        other = (z + NZ - i) % NZ
        return remote(lgat.at[other], lgat.at[other], lz_send.at[i], lz_recv.at[i], at_z(i))

    for i in range(1, NY):
        lse_y(i).start()

    def backward(group, slot0, count, first):
        n = count * TOK
        tr[:, :n] = kv[slot0 : slot0 + count, 0].reshape(n, D).T
        values = kv[slot0 : slot0 + count, 1].reshape(n, D)

        def step(c, carry):
            cols = chunk_of(c)
            share = jnp.exp2(mgrp[group : group + 1, cols] - mrun[:, cols]) / lrun[:, cols]
            p = pbuf[slot0 * TOK : slot0 * TOK + n, cols].astype(F32) * share
            dp = dot(values, gt[:, cols])
            ds = (p * (dp - delta[:, cols])).astype(BF16)
            plb[:n, cols] = p.astype(BF16)
            dsb[:n, cols] = ds
            dq = dot(tr[:, :n], ds)
            if first:
                dqt[:, cols] = dq
            else:
                dqt[:, cols] += dq
            return carry

        lax.fori_loop(0, NCHUNK, step, 0)
        part[slot0 : slot0 + count, 0] = dot(dsb[:n, :], qs[...]).astype(BF16).reshape(count, TOK, D)
        part[slot0 : slot0 + count, 1] = dot(plb[:n, :], gs[...]).astype(BF16).reshape(count, TOK, D)

    def grad_y(g, i):
        other = (y + i) % NY
        return remote(
            part.at[4 * g + other], yrecv.at[g, y], gy_send.at[3 * g + i - 1],
            gy_recv.at[4 * g + y], at_y(i),
        )

    def grad_y_goes(g, i):
        return ((y + i) >= NY) | (z >= 4) if g == 3 else z >= g + 1

    def grad_y_start(g):
        for i in range(1, NY):

            @pl.when(grad_y_goes(g, i))
            def _(i=i):
                grad_y(g, i).start()

    def grad_y_arrival(g, other):
        remote(
            yrecv.at[g, other], yrecv.at[g, other], gy_send.at[0], gy_recv.at[4 * g + other], at_y(1)
        ).wait_recv()

    def grad_z(level):
        to = (jnp.maximum(z - 1, 0) * NY + y, head)
        return remote(
            zsend.at[level - 1], zrecv.at[level - 1], gz_send.at[level - 1], gz_recv.at[level - 1], to
        )

    def wide(ref, *at):
        return ref[at].astype(F32)

    def reduce_level(level):
        g = level - 1

        @pl.when(z >= level)
        def _():
            total[...] = wide(part, 4 * g + y)
            for i in range(1, NY):
                other = (y + i) % NY
                if level == 4:

                    @pl.when(other < y)
                    def _(other=other):
                        grad_y_arrival(g, other)
                        total[...] += wide(yrecv, g, other)
                else:
                    grad_y_arrival(g, other)
                    total[...] += wide(yrecv, g, other)
            if level < 4:

                @pl.when(z < NZ - 1)
                def _():
                    grad_z(level + 1).wait_recv()
                    total[...] += wide(zrecv, level)

            zsend[level - 1] = total[...].astype(BF16)
            grad_z(level).start()

    backward(4, 12, 4, True)
    grad_y_start(3)
    for i in range(1, NY):
        lse_y_arrival(i).wait_recv()
    for i in range(1, NZ):
        lse_z(i).start()
    for level in (3, 2, 1):

        @pl.when(z >= level)
        def _(level=level):
            backward(level, 4 * (level - 1), 4, False)

        grad_y_start(level - 1)
        reduce_level(level + 1)
    backward(0, OWN, 1, False)
    reduce_level(1)
    total[...] = wide(part, OWN)
    for i in range(1, NY):
        other = (y + i) % NY

        @pl.when(other > y)
        def _(other=other):
            grad_y_arrival(3, other)
            total[...] += wide(yrecv, 3, other)

    for h in range(HG):
        cols = slice(h * D, (h + 1) * D)
        att_ref[:, cols] = ot[:, cols].T.astype(BF16)
        gq_ref[:, cols] = (dqt[:, cols] * SCALE).T.astype(BF16)

    for i in range(1, NZ):
        lse_z_arrival(i).wait_recv()
    lane = lax.broadcasted_iota(jnp.int32, (HG, TOK), 1) // 4
    owned = jnp.zeros((HG, TOK), F32)
    for d in range(NZ * NY):
        moved = pltpu.roll(lgat[d // NY, d % NY], ((d - ctx) * 4) % TOK, 1)
        owned = jnp.where(lane == d, moved, owned)
    lse_ref[...] = owned

    @pl.when(z < NZ - 1)
    def _():
        grad_z(1).wait_recv()
        total[...] += wide(zrecv, 0)

    part[OWN, 0] = (total[0] * SCALE).astype(BF16)
    part[OWN, 1] = total[1].astype(BF16)

    def home(i):
        rows = pl.ds(pl.multiple_of(((head + i) % NH) * TOKDEV, TOKDEV), TOKDEV)
        return remote(
            part.at[OWN, :, rows, :], hrecv.at[head], hb_send.at[i], hb_recv.at[i], at_head(i)
        )

    def home_arrival(i):
        other = (head + NH - i) % NH
        return remote(hrecv.at[other], hrecv.at[other], hb_send.at[i], hb_recv.at[i], at_head(i))

    for i in range(1, NH):
        home(i).start()
    hrecv[head] = part[OWN, :, pl.ds(pl.multiple_of(head * TOKDEV, TOKDEV), TOKDEV), :]

    for i in range(1, NH):
        head_copy(i).wait_send()
    for hop in range(1, 5):

        @pl.when(chain_goes(hop))
        def _(hop=hop):
            chain_copy(hop).wait_send()

        @pl.when(z >= hop)
        def _(hop=hop):
            grad_z(hop).wait_send()

    for level in range(5):
        for i in range(1, NY):

            @pl.when(spread_goes(level, i))
            def _(level=level, i=i):
                spread_copy(level, i).wait_send()

    for g in range(4):
        for i in range(1, NY):

            @pl.when(grad_y_goes(g, i))
            def _(g=g, i=i):
                grad_y(g, i).wait_send()

    for i in range(1, NY):
        lse_y(i).wait_send()
    for i in range(1, NZ):
        lse_z(i).wait_send()
    for i in range(1, NH):
        home_arrival(i).wait_recv()
    for h in range(NH):
        gk_ref[:, h * D : (h + 1) * D] = hrecv[h, 0]
        gv_ref[:, h * D : (h + 1) * D] = hrecv[h, 1]
    for i in range(1, NH):
        home(i).wait_send()


def body(queries, key_rows, value_rows, grad_out, doc_ids, block_owner):
    vmem = pl.BlockSpec(memory_space=pltpu.VMEM)
    anywhere = pl.BlockSpec(memory_space=pl.ANY)
    dma = pltpu.SemaphoreType.DMA
    keys = 17 * TOK
    return pl.pallas_call(
        kernel,
        out_shape=(
            jax.ShapeDtypeStruct((TOK, ROWS), BF16),
            jax.ShapeDtypeStruct((HG, TOK), F32),
            jax.ShapeDtypeStruct((TOK, ROWS), BF16),
            jax.ShapeDtypeStruct((TOKDEV, NH * D), BF16),
            jax.ShapeDtypeStruct((TOKDEV, NH * D), BF16),
        ),
        in_specs=[anywhere, vmem, vmem, anywhere, vmem, vmem],
        out_specs=(vmem,) * 5,
        scratch_shapes=[
            pltpu.VMEM((TOK, ROWS), BF16),
            pltpu.VMEM((TOK, ROWS), BF16),
            pltpu.VMEM((D, ROWS), BF16),
            pltpu.VMEM((D, ROWS), BF16),
            pltpu.VMEM((ROWS, D), BF16),
            pltpu.VMEM((ROWS, D), BF16),
            pltpu.VMEM((17, 2, TOK, D), BF16),
            pltpu.VMEM((NH, 2, TOKDEV, D), BF16),
            pltpu.VMEM((keys, ROWS), BF16),
            pltpu.VMEM((4 * TOK, ROWS), BF16),
            pltpu.VMEM((4 * TOK, ROWS), BF16),
            pltpu.VMEM((D, 4 * TOK), BF16),
            pltpu.VMEM((D, ROWS), F32),
            pltpu.VMEM((D, ROWS), F32),
            pltpu.VMEM((1, ROWS), F32),
            pltpu.VMEM((1, ROWS), F32),
            pltpu.VMEM((8, ROWS), F32),
            pltpu.VMEM((1, ROWS), F32),
            pltpu.VMEM((17, 2, TOK, D), BF16),
            pltpu.VMEM((4, NY, 2, TOK, D), BF16),
            pltpu.VMEM((4, 2, TOK, D), BF16),
            pltpu.VMEM((4, 2, TOK, D), BF16),
            pltpu.VMEM((2, TOK, D), F32),
            pltpu.VMEM((NH, 2, TOKDEV, D), BF16),
            pltpu.VMEM((HG, TOK), F32),
            pltpu.VMEM((NZ, NY, HG, TOK), F32),
            dma((2,)),
            dma((NH,)), dma((NH,)),
            dma((4,)), dma((15,)), dma((17,)),
            dma((12,)), dma((16,)), dma((4,)), dma((4,)),
            dma((NH,)), dma((NH,)),
            dma((NY,)), dma((NY,)), dma((NZ,)), dma((NZ,)),
        ],
        compiler_params=pltpu.CompilerParams(
            collective_id=0, has_side_effects=True, vmem_limit_bytes=48 * 1024 * 1024
        ),
        name="packed_attention",
    )(queries, key_rows, value_rows, grad_out, doc_ids.reshape(32, TOK), block_owner)


def solution(mesh):
    return jax.shard_map(
        body,
        mesh=mesh,
        in_specs=(
            P("ctx", "head"), P(("ctx", "head"), None), P(("ctx", "head"), None),
            P("ctx", "head"), P(), P(),
        ),
        out_specs=(
            P("ctx", "head"), P("head", "ctx"), P("ctx", "head"),
            P(("ctx", "head"), None), P(("ctx", "head"), None),
        ),
        check_vma=False,
    )
```

```python
import functools

import jax
import jax.numpy as jnp
from jax import lax
from jax.experimental import pallas as pl
from jax.experimental.pallas import tpu as pltpu
from jax.sharding import PartitionSpec as P

D = 128
TOK = 128
HG = 8
ROWS = HG * TOK
CHUNK = 256
NCHUNK = ROWS // CHUNK
NZ, NY = 8, 4
NH = 8
TOKDEV = 16
OWN = 16
LOG2E = 1.4426950408889634
LN2 = 0.6931471805599453
NEG = -1e30
SCALE = D**-0.5
F32 = jnp.float32
BF16 = jnp.bfloat16
MESH = pl.DeviceIdType.MESH


def dot(a, b):
    return jnp.dot(a, b, preferred_element_type=F32)


def kernel(
    q_hbm, k_hbm, v_hbm, g_hbm, doc_hbm, owner_hbm,
    att_ref, lse_ref, gq_ref, gk_ref, gv_ref,
    q_in, g_in, k_ref, v_ref, doc_ref, owner_ref,
    qt, gt, qs, gs, kv, stage, pbuf, dpb, dsb, kt, tr, ot, dqt, mrun, lrun, mgrp, delta,
    part, yrecv, zrecv, zsend, total, pieces, hrecv, lown, lgat,
    load_sem, ha_send, ha_recv, kz_send, ky_send, kv_recv,
    gy_send, gy_recv, gz_send, gz_recv, hb_send, hb_recv, ly_send, ly_recv, lz_send, lz_recv,
):
    ctx = lax.axis_index("ctx")
    head = lax.axis_index("head")
    z = ctx // NY
    y = ctx % NY

    loads = [
        pltpu.make_async_copy(src, dst, load_sem.at[i])
        for i, (src, dst) in enumerate(
            (
                (k_hbm, k_ref), (v_hbm, v_ref), (q_hbm, q_in), (g_hbm, g_in),
                (doc_hbm, doc_ref), (owner_hbm, owner_ref),
            )
        )
    ]
    for load in loads:
        load.start()

    def at_head(i):
        return (ctx, (head + i) % NH)

    def at_y(i):
        return (z * NY + (y + i) % NY, head)

    def at_z(i):
        return (((z + i) % NZ) * NY + y, head)

    barrier = pltpu.get_barrier_semaphore()
    for i in range(1, NH):
        pl.semaphore_signal(barrier, inc=1, device_id=at_head(i), device_id_type=MESH)
    for i in range(1, NY):
        pl.semaphore_signal(barrier, inc=1, device_id=at_y(i), device_id_type=MESH)
    for i in (1, NZ - 1):
        pl.semaphore_signal(barrier, inc=1, device_id=at_z(i), device_id_type=MESH)

    loads[0].wait()
    loads[1].wait()
    for h in range(NH):
        stage[h, 0] = k_ref[:, h * D : (h + 1) * D]
        stage[h, 1] = v_ref[:, h * D : (h + 1) * D]
    pl.semaphore_wait(barrier, NH + NY)

    def remote(src, dst, ssem, rsem, to):
        return pltpu.make_async_remote_copy(
            src_ref=src, dst_ref=dst, send_sem=ssem, recv_sem=rsem, device_id=to, device_id_type=MESH
        )

    def head_copy(i):
        to = (head + i) % NH
        rows = pl.ds(pl.multiple_of(head * TOKDEV, TOKDEV), TOKDEV)
        return remote(
            stage.at[to], kv.at[OWN, :, rows, :], ha_send.at[i], ha_recv.at[i], at_head(i)
        )

    def head_arrival(i):
        rows = pl.ds(pl.multiple_of(((head + NH - i) % NH) * TOKDEV, TOKDEV), TOKDEV)
        return remote(stage.at[0], kv.at[OWN, :, rows, :], ha_send.at[i], ha_recv.at[i], at_head(i))

    for i in range(1, NH):
        head_copy(i).start()
    kv[OWN, :, pl.ds(pl.multiple_of(head * TOKDEV, TOKDEV), TOKDEV), :] = stage[head]

    for load in loads[2:]:
        load.wait()
    for h in range(HG):
        cols = slice(h * D, (h + 1) * D)
        qh, gh = q_in[:, cols], g_in[:, cols]
        qs[cols, :] = qh
        gs[cols, :] = gh
        qt[:, cols] = qh.T
        gt[:, cols] = gh.T

    @pl.when(z < 4)
    def _():
        for j in range(NY):

            @pl.when(y <= j)
            def _(j=j):
                kv[12 + j] = jnp.zeros((2, TOK, D), BF16)

    for i in range(1, NH):
        head_arrival(i).wait_recv()

    def chain_copy(hop):
        src = kv.at[OWN] if hop == 1 else kv.at[4 * (hop - 2) + y]
        dst = kv.at[4 * (hop - 1) + y]
        to = (jnp.minimum(z + 1, NZ - 1) * NY + y, head)
        return remote(src, dst, kz_send.at[hop - 1], kv_recv.at[4 * (hop - 1) + y], to)

    def chain_goes(hop):
        return (z < NZ - 1) & (z >= hop - 1)

    def chain_start(hop):
        @pl.when(chain_goes(hop))
        def _():
            chain_copy(hop).start()

    def spread_copy(level, i):
        src = kv.at[OWN] if level == 0 else kv.at[4 * (level - 1) + y]
        slot = 12 + y if level in (0, 4) else 4 * (level - 1) + y
        return remote(src, kv.at[slot], ky_send.at[3 * level + i - 1], kv_recv.at[slot], at_y(i))

    def spread_goes(level, i):
        if level == 0:
            return (y + i) < NY
        if level == 4:
            return (z >= 4) & ((y + i) >= NY)
        return z >= level

    def spread_start(level):
        for i in range(1, NY):

            @pl.when(spread_goes(level, i))
            def _(i=i):
                spread_copy(level, i).start()

    def slot_arrival(slot):
        remote(kv.at[slot], kv.at[slot], kz_send.at[0], kv_recv.at[slot], at_y(1)).wait_recv()

    chain_start(1)
    spread_start(0)

    docs = doc_ref[...]
    mine = doc_ref[pl.ds(ctx, 1), :]
    starts = jnp.zeros((1, TOK), F32)
    for v in range(1, 4):
        below = jnp.where(docs < v, 1.0, 0.0).astype(F32)
        count = jnp.sum(jnp.sum(below, axis=0, keepdims=True), axis=1, keepdims=True)
        starts = jnp.where(mine == v, count, starts)
    starts = jnp.concatenate([starts, starts], axis=1)
    tpos = lax.broadcasted_iota(jnp.int32, (1, TOK), 1).astype(F32)
    tpos = jnp.concatenate([tpos, tpos], axis=1) + (ctx * TOK).astype(F32)

    def positions(bases):
        step = lax.broadcasted_iota(jnp.int32, (TOK, 1), 0).astype(F32)
        return jnp.concatenate([step + b.astype(F32) for b in bases], axis=0)

    def chunk_of(c):
        return slice(c * CHUNK, (c + 1) * CHUNK)

    def forward(group, slot0, count, bases, diagonal, halfway=None):
        n = count * TOK
        span = slice(slot0 * TOK, slot0 * TOK + n)
        keys = kv[slot0 : slot0 + count, 0].reshape(n, D)
        values = kv[slot0 : slot0 + count, 1].reshape(n, D)
        kt[:, span] = keys.T
        tr[:, :n] = values.T
        kpos = positions(bases)

        def step(c):
            cols = chunk_of(c)
            s = dot(keys, qt[:, cols]) * (SCALE * LOG2E)
            allowed = kpos >= starts
            if diagonal:
                allowed = allowed & (kpos <= tpos)
            s = jnp.where(allowed, s, NEG)
            top = jnp.max(s, axis=0, keepdims=True)
            if not diagonal:
                before = mrun[:, cols]
                top = jnp.maximum(before, top)
                fade = jnp.exp2(before - top)
            p = jnp.exp2(s - top)
            mass = jnp.sum(p, axis=0, keepdims=True)
            low = p.astype(BF16)
            pbuf[span, cols] = low
            part_o = dot(tr[:, :n], low)
            dpb[span, cols] = dot(values, gt[:, cols])
            if diagonal:
                lrun[:, cols] = mass
                ot[:, cols] = part_o
            else:
                lrun[:, cols] = lrun[:, cols] * fade + mass
                ot[:, cols] = ot[:, cols] * fade + part_o
            mrun[:, cols] = top
            mgrp[group : group + 1, cols] = top
            if halfway is not None and c == NCHUNK // 2 - 1:
                halfway()

        for c in range(NCHUNK):
            step(c)

    def level_bases(level):
        return [((z - level) * NY + j) * TOK for j in range(NY)]

    mix_bases = [jnp.where(j < y, z * NY + j, (z - 4) * NY + j) * TOK for j in range(NY)]

    def pass_on(level):
        @pl.when(z >= level)
        def _():
            slot_arrival(4 * (level - 1) + y)

        if level < 4:
            chain_start(level + 1)
        spread_start(level)

    def await_level(level):
        @pl.when(z >= level)
        def _():
            for i in range(1, NY):
                slot_arrival(4 * (level - 1) + (y + i) % NY)

    forward(0, OWN, 1, [ctx * TOK], True)
    pass_on(1)
    pass_on(2)
    for level in (1, 2, 3):
        await_level(level)
        if level < 3:
            halfway = functools.partial(pass_on, level + 2)

            @pl.when(z < level)
            def _(halfway=halfway):
                halfway()

        else:
            halfway = None

        @pl.when(z >= level)
        def _(level=level, halfway=halfway):
            forward(level, 4 * (level - 1), 4, level_bases(level), False, halfway)

    for i in range(1, NY):
        other = (y + i) % NY

        @pl.when((other < y) | (z >= 4))
        def _(other=other):
            slot_arrival(12 + other)

    forward(4, 12, 4, mix_bases, False)

    def finish(c):
        cols = chunk_of(c)
        mass = lrun[:, cols]
        out = (ot[:, cols] / mass).astype(BF16)
        wide = out.astype(F32)
        ot[:, cols] = wide
        delta[:, cols] = jnp.sum(gt[:, cols].astype(F32) * wide, axis=0, keepdims=True)

    for c in range(NCHUNK):
        finish(c)
    norm = mrun[...] * LN2 + jnp.log(lrun[...])
    for h in range(HG):
        cols = slice(h * D, (h + 1) * D)
        lown[h : h + 1, :] = norm[:, cols]
    reps = lax.broadcasted_iota(jnp.int32, (32, TOK), 1) // 4 == lax.broadcasted_iota(
        jnp.int32, (32, TOK), 0
    )
    owners = dot(owner_ref[pl.ds(ctx, 1), :].astype(F32), jnp.where(reps, 1.0, 0.0).astype(F32))
    to_col = lax.broadcasted_iota(jnp.int32, (TOK, TOK), 0)
    from_tok = lax.broadcasted_iota(jnp.int32, (TOK, TOK), 1)
    hit = (owners == (to_col // 4).astype(F32)) & (to_col % 4 == from_tok % 4)
    lgat[z, y] = lax.dot_general(
        lown[...],
        jnp.where(hit, 1.0, 0.0).astype(F32),
        (((1,), (1,)), ((), ())),
        precision=lax.Precision.HIGHEST,
        preferred_element_type=F32,
    )

    def lse_y(i):
        return remote(lgat.at[z, y], lgat.at[z, y], ly_send.at[i], ly_recv.at[i], at_y(i))

    def lse_y_arrival(i):
        other = (y + NY - i) % NY
        return remote(lgat.at[z, other], lgat.at[z, other], ly_send.at[i], ly_recv.at[i], at_y(i))

    def lse_up(step):
        block = lgat.at[(z + NZ - step) % NZ]
        return remote(block, block, lz_send.at[step], lz_recv.at[step], at_z(1))

    def lse_up_arrival(step):
        block = lgat.at[(z + NZ - 1 - step) % NZ]
        return remote(block, block, lz_send.at[step], lz_recv.at[step], at_z(1))

    def lse_down(step):
        block = lgat.at[(z + step) % NZ]
        return remote(block, block, lz_send.at[4 + step], lz_recv.at[4 + step], at_z(NZ - 1))

    def lse_down_arrival(step):
        block = lgat.at[(z + 1 + step) % NZ]
        return remote(block, block, lz_send.at[4 + step], lz_recv.at[4 + step], at_z(NZ - 1))

    def lse_step(step):
        if step == 0:
            for i in range(1, NY):
                lse_y_arrival(i).wait_recv()
        else:
            lse_up_arrival(step - 1).wait_recv()
            if step < 4:
                lse_down_arrival(step - 1).wait_recv()
        if step < 4:
            lse_up(step).start()
        if step < 3:
            lse_down(step).start()

    for i in range(1, NY):
        lse_y(i).start()

    def backward(group, slot0, count):
        n = count * TOK
        span = slice(slot0 * TOK, slot0 * TOK + n)

        def step(c):
            cols = chunk_of(c)
            share = jnp.exp2(mgrp[group : group + 1, cols] - mrun[:, cols]) / lrun[:, cols]
            p = pbuf[span, cols].astype(F32) * share
            dsb[span, cols] = (p * (dpb[span, cols] - delta[:, cols])).astype(BF16)
            pbuf[span, cols] = p.astype(BF16)

        for c in range(NCHUNK):
            step(c)
        part[slot0 : slot0 + count, 0] = dot(dsb[span, :], qs[...]).astype(BF16).reshape(count, TOK, D)
        part[slot0 : slot0 + count, 1] = dot(pbuf[span, :], gs[...]).astype(BF16).reshape(count, TOK, D)

    def query_gradient(slot0, count, first):
        span = slice(slot0 * TOK, (slot0 + count) * TOK)

        def step(c):
            cols = chunk_of(c)
            dq = dot(kt[:, span], dsb[span, cols])
            if first:
                dqt[:, cols] = dq
            else:
                dqt[:, cols] += dq

        for c in range(NCHUNK):
            step(c)

    def grad_y(g, i):
        other = (y + i) % NY
        return remote(
            part.at[4 * g + other], yrecv.at[g, y], gy_send.at[3 * g + i - 1],
            gy_recv.at[4 * g + y], at_y(i),
        )

    def grad_y_goes(g, i, part_of=None):
        if g < 3:
            return z >= g + 1
        own_level, far_level = (y + i) >= NY, ((y + i) < NY) & (z >= 4)
        return {None: own_level | far_level, 0: own_level, 4: far_level}[part_of]

    def grad_y_start(g, part_of=None):
        for i in range(1, NY):

            @pl.when(grad_y_goes(g, i, part_of))
            def _(i=i):
                grad_y(g, i).start()

    def grad_y_arrival(g, other):
        remote(
            yrecv.at[g, other], yrecv.at[g, other], gy_send.at[0], gy_recv.at[4 * g + other], at_y(1)
        ).wait_recv()

    def wide(ref, *at):
        return ref[at].astype(F32)

    def grad_z(level):
        to = (jnp.maximum(z - (1 if level == 3 else 2), 0) * NY + y, head)
        at = level - 2
        return remote(zsend.at[at], zrecv.at[at], gz_send.at[at], gz_recv.at[at], to)

    def column_sum(level):
        g = level - 1
        total[...] = wide(part, 4 * g + y)
        for i in range(1, NY):
            other = (y + i) % NY
            if level == 4:

                @pl.when(other < y)
                def _(other=other):
                    grad_y_arrival(g, other)
                    total[...] += wide(yrecv, g, other)
            else:
                grad_y_arrival(g, other)
                total[...] += wide(yrecv, g, other)

    def from_z(level):
        grad_z(level).wait_recv()
        total[...] += wide(zrecv, level - 2)

    def reduce_level(level):
        @pl.when(z >= level)
        def _():
            column_sum(level)
            if level == 2:
                pl.when(z < NZ - 2)(lambda: from_z(4))
                pl.when(z < NZ - 1)(lambda: from_z(3))
            zsend[level - 2] = total[...].astype(BF16)
            grad_z(level).start()

    def home_rows(to):
        return pl.ds(pl.multiple_of(to * TOKDEV, TOKDEV), TOKDEV)

    def home(i):
        return remote(
            pieces.at[0, :, home_rows((head + i) % NH), :], hrecv.at[0, head],
            hb_send.at[0, i], hb_recv.at[0, i], at_head(i),
        )

    def home_arrival(i):
        ref = hrecv.at[0, (head + NH - i) % NH]
        return remote(ref, ref, hb_send.at[0, i], hb_recv.at[0, i], at_head(i))

    def home_down(i):
        to = (head + i) % NH
        return remote(
            pieces.at[1, :, home_rows(to), :], hrecv.at[1, head],
            hb_send.at[1, i], hb_recv.at[1, i], (jnp.maximum(z - 1, 0) * NY + y, to),
        )

    def home_down_arrival(i):
        ref = hrecv.at[1, (head + NH - i) % NH]
        return remote(ref, ref, hb_send.at[1, i], hb_recv.at[1, i], at_head(i))

    def leave(at):
        pieces[at, 0] = (total[0] * SCALE).astype(BF16)
        pieces[at, 1] = total[1].astype(BF16)

    def at_level(level, fn, *args):
        pl.when(z >= level)(lambda: fn(*args))

    backward(4, 12, 4)
    grad_y_start(3, 4)
    at_level(3, backward, 3, 8, 4)
    grad_y_start(2)
    lse_step(0)
    at_level(2, backward, 2, 4, 4)
    grad_y_start(1)
    at_level(1, backward, 1, 0, 4)
    grad_y_start(0)
    grad_y_start(3, 0)
    reduce_level(4)
    lse_step(1)
    backward(0, OWN, 1)
    query_gradient(OWN, 1, True)
    reduce_level(3)
    lse_step(2)
    query_gradient(12, 4, False)
    at_level(3, query_gradient, 8, 4, False)
    lse_step(3)
    reduce_level(2)
    at_level(2, query_gradient, 4, 4, False)
    at_level(1, query_gradient, 0, 4, False)
    for h in range(HG):
        cols = slice(h * D, (h + 1) * D)
        att_ref[:, cols] = ot[:, cols].T.astype(BF16)
        gq_ref[:, cols] = (dqt[:, cols] * SCALE).T.astype(BF16)

    @pl.when(z >= 1)
    def _():
        column_sum(1)
        leave(1)
        for i in range(NH):
            home_down(i).start()

    total[...] = wide(part, OWN)
    for i in range(1, NY):
        other = (y + i) % NY

        @pl.when(other > y)
        def _(other=other):
            grad_y_arrival(3, other)
            total[...] += wide(yrecv, 3, other)

    pl.when(z < NZ - 2)(lambda: from_z(2))
    leave(0)
    for i in range(1, NH):
        home(i).start()
    hrecv[0, head] = pieces[0, :, home_rows(head), :]

    lse_step(4)
    lane = lax.broadcasted_iota(jnp.int32, (HG, TOK), 1) // 4
    owned = jnp.zeros((HG, TOK), F32)
    for d in range(NZ * NY):
        moved = pltpu.roll(lgat[d // NY, d % NY], ((d - ctx) * 4) % TOK, 1)
        owned = jnp.where(lane == d, moved, owned)
    lse_ref[...] = owned

    for i in range(1, NH):
        head_copy(i).wait_send()
    for hop in range(1, 5):

        @pl.when(chain_goes(hop))
        def _(hop=hop):
            chain_copy(hop).wait_send()

        if hop > 1:

            @pl.when(z >= hop)
            def _(hop=hop):
                grad_z(hop).wait_send()

    for level in range(5):
        for i in range(1, NY):

            @pl.when(spread_goes(level, i))
            def _(level=level, i=i):
                spread_copy(level, i).wait_send()

    for g in range(4):
        for i in range(1, NY):

            @pl.when(grad_y_goes(g, i))
            def _(g=g, i=i):
                grad_y(g, i).wait_send()

    for i in range(1, NY):
        lse_y(i).wait_send()
    for step in range(4):
        lse_up(step).wait_send()
    for step in range(3):
        lse_down(step).wait_send()

    @pl.when(z == NZ - 1)
    def _():
        hrecv[1] = jnp.zeros((NH, 2, TOKDEV, D), BF16)

    @pl.when(z < NZ - 1)
    def _():
        for i in range(NH):
            home_down_arrival(i).wait_recv()

    for i in range(1, NH):
        home_arrival(i).wait_recv()
    for h in range(NH):
        cols = slice(h * D, (h + 1) * D)
        both = wide(hrecv, 0, h) + wide(hrecv, 1, h)
        gk_ref[:, cols] = both[0].astype(BF16)
        gv_ref[:, cols] = both[1].astype(BF16)

    @pl.when(z >= 1)
    def _():
        for i in range(NH):
            home_down(i).wait_send()

    for i in range(1, NH):
        home(i).wait_send()


def deliver(*refs):
    sem = refs[-1]
    copies = [pltpu.make_async_copy(refs[i], refs[5 + i], sem.at[i]) for i in range(5)]
    for copy in copies:
        copy.start()
    for copy in copies:
        copy.wait()


def body(queries, key_rows, value_rows, grad_out, doc_ids, block_owner):
    vmem = pl.BlockSpec(memory_space=pltpu.VMEM)
    hbm = pl.BlockSpec(memory_space=pltpu.HBM)
    dma = pltpu.SemaphoreType.DMA
    keys = 17 * TOK
    shapes = (
        jax.ShapeDtypeStruct((TOK, ROWS), BF16),
        jax.ShapeDtypeStruct((HG, TOK), F32),
        jax.ShapeDtypeStruct((TOK, ROWS), BF16),
        jax.ShapeDtypeStruct((TOKDEV, NH * D), BF16),
        jax.ShapeDtypeStruct((TOKDEV, NH * D), BF16),
    )
    outs = pl.pallas_call(
        kernel,
        out_shape=shapes,
        in_specs=[hbm] * 6,
        out_specs=(vmem,) * 5,
        scratch_shapes=[
            pltpu.VMEM((TOK, ROWS), BF16),
            pltpu.VMEM((TOK, ROWS), BF16),
            pltpu.VMEM((TOKDEV, NH * D), BF16),
            pltpu.VMEM((TOKDEV, NH * D), BF16),
            pltpu.VMEM((32, TOK), jnp.int32),
            pltpu.VMEM((32, 32), jnp.int32),
            pltpu.VMEM((D, ROWS), BF16),
            pltpu.VMEM((D, ROWS), BF16),
            pltpu.VMEM((ROWS, D), BF16),
            pltpu.VMEM((ROWS, D), BF16),
            pltpu.VMEM((17, 2, TOK, D), BF16),
            pltpu.VMEM((NH, 2, TOKDEV, D), BF16),
            pltpu.VMEM((keys, ROWS), BF16),
            pltpu.VMEM((keys, ROWS), F32),
            pltpu.VMEM((keys, ROWS), BF16),
            pltpu.VMEM((D, keys), BF16),
            pltpu.VMEM((D, 4 * TOK), BF16),
            pltpu.VMEM((D, ROWS), F32),
            pltpu.VMEM((D, ROWS), F32),
            pltpu.VMEM((1, ROWS), F32),
            pltpu.VMEM((1, ROWS), F32),
            pltpu.VMEM((8, ROWS), F32),
            pltpu.VMEM((1, ROWS), F32),
            pltpu.VMEM((17, 2, TOK, D), BF16),
            pltpu.VMEM((4, NY, 2, TOK, D), BF16),
            pltpu.VMEM((3, 2, TOK, D), BF16),
            pltpu.VMEM((3, 2, TOK, D), BF16),
            pltpu.VMEM((2, TOK, D), F32),
            pltpu.VMEM((2, 2, TOK, D), BF16),
            pltpu.VMEM((2, NH, 2, TOKDEV, D), BF16),
            pltpu.VMEM((HG, TOK), F32),
            pltpu.VMEM((NZ, NY, HG, TOK), F32),
            dma((6,)),
            dma((NH,)), dma((NH,)),
            dma((4,)), dma((15,)), dma((17,)),
            dma((12,)), dma((16,)), dma((3,)), dma((3,)),
            dma((2, NH)), dma((2, NH)),
            dma((NY,)), dma((NY,)), dma((NZ,)), dma((NZ,)),
        ],
        compiler_params=pltpu.CompilerParams(
            collective_id=0, has_side_effects=True, vmem_limit_bytes=60 * 1024 * 1024
        ),
        name="packed_attention",
    )(queries, key_rows, value_rows, grad_out, doc_ids.reshape(32, TOK), block_owner)
    return pl.pallas_call(
        deliver,
        out_shape=shapes,
        in_specs=[vmem] * 5,
        out_specs=(hbm,) * 5,
        scratch_shapes=[dma((5,))],
        name="deliver",
    )(*outs)


def solution(mesh):
    return jax.shard_map(
        body,
        mesh=mesh,
        in_specs=(
            P("ctx", "head"), P(("ctx", "head"), None), P(("ctx", "head"), None),
            P("ctx", "head"), P(), P(),
        ),
        out_specs=(
            P("ctx", "head"), P("head", "ctx"), P("ctx", "head"),
            P(("ctx", "head"), None), P(("ctx", "head"), None),
        ),
        check_vma=False,
    )
```

```python
import jax
import jax.numpy as jnp
from jax import lax
from jax.experimental import pallas as pl
from jax.experimental.pallas import tpu as pltpu
from jax.sharding import PartitionSpec as P

D = 128
TOK = 128
HG = 8
ROWS = HG * TOK
CHUNK = 256
NCHUNK = ROWS // CHUNK
NZ, NY = 8, 4
NH = 8
TOKDEV = 16
OWN = 16
LOG2E = 1.4426950408889634
LN2 = 0.6931471805599453
NEG = -1e30
SCALE = D**-0.5
F32 = jnp.float32
BF16 = jnp.bfloat16
MESH = pl.DeviceIdType.MESH


def dot(a, b):
    return jnp.dot(a, b, preferred_element_type=F32)


def kernel(
    q_hbm, k_hbm, v_hbm, g_hbm, doc_hbm, owner_hbm,
    att_hbm, lse_hbm, gq_hbm, gk_hbm, gv_hbm,
    q_in, g_in, k_ref, v_ref, doc_ref, owner_ref,
    att_ref, lse_ref, gq_ref, gk_ref, gv_ref, store_sem,
    qt, gt, qs, gs, kv, stage, pbuf, dpb, dsb, kt, tr, ot, dqt, mrun, lrun, mgrp, delta,
    part, yrecv, zrecv, zsend, total, pieces, hrecv, lown, lgat,
    load_sem, ha_send, ha_recv, kz_send, ky_send, kv_recv,
    gy_send, gy_recv, gz_send, gz_recv, hb_send, hb_recv, ly_send, ly_recv, lz_send, lz_recv,
):
    ctx = lax.axis_index("ctx")
    head = lax.axis_index("head")
    z = ctx // NY
    y = ctx % NY

    loads = [
        pltpu.make_async_copy(src, dst, load_sem.at[i])
        for i, (src, dst) in enumerate(
            (
                (k_hbm, k_ref), (v_hbm, v_ref), (q_hbm, q_in), (g_hbm, g_in),
                (doc_hbm, doc_ref), (owner_hbm, owner_ref),
            )
        )
    ]
    for load in loads:
        load.start()

    stores = [
        pltpu.make_async_copy(src, dst, store_sem.at[i])
        for i, (src, dst) in enumerate(
            (
                (att_ref, att_hbm), (gq_ref, gq_hbm), (lse_ref, lse_hbm),
                (gk_ref, gk_hbm), (gv_ref, gv_hbm),
            )
        )
    ]

    def at_head(i):
        return (ctx, (head + i) % NH)

    def at_y(i):
        return (z * NY + (y + i) % NY, head)

    def at_z(i):
        return (((z + i) % NZ) * NY + y, head)

    barrier = pltpu.get_barrier_semaphore()
    for i in range(1, NH):
        pl.semaphore_signal(barrier, inc=1, device_id=at_head(i), device_id_type=MESH)
    for i in range(1, NY):
        pl.semaphore_signal(barrier, inc=1, device_id=at_y(i), device_id_type=MESH)
    for i in (1, 2, 4, 6, 7):
        pl.semaphore_signal(barrier, inc=1, device_id=at_z(i), device_id_type=MESH)

    loads[0].wait()
    loads[1].wait()
    for h in range(NH):
        stage[h, 0] = k_ref[:, h * D : (h + 1) * D]
        stage[h, 1] = v_ref[:, h * D : (h + 1) * D]
    pl.semaphore_wait(barrier, NH + NY + 3)

    def remote(src, dst, ssem, rsem, to):
        return pltpu.make_async_remote_copy(
            src_ref=src, dst_ref=dst, send_sem=ssem, recv_sem=rsem, device_id=to, device_id_type=MESH
        )

    def head_copy(i):
        to = (head + i) % NH
        rows = pl.ds(pl.multiple_of(head * TOKDEV, TOKDEV), TOKDEV)
        return remote(
            stage.at[to], kv.at[OWN, :, rows, :], ha_send.at[i], ha_recv.at[i], at_head(i)
        )

    def head_arrival(i):
        rows = pl.ds(pl.multiple_of(((head + NH - i) % NH) * TOKDEV, TOKDEV), TOKDEV)
        return remote(stage.at[0], kv.at[OWN, :, rows, :], ha_send.at[i], ha_recv.at[i], at_head(i))

    for i in range(1, NH):
        head_copy(i).start()
    kv[OWN, :, pl.ds(pl.multiple_of(head * TOKDEV, TOKDEV), TOKDEV), :] = stage[head]

    for load in loads[2:]:
        load.wait()
    for h in range(HG):
        cols = slice(h * D, (h + 1) * D)
        qh, gh = q_in[:, cols], g_in[:, cols]
        qs[cols, :] = qh
        gs[cols, :] = gh
        qt[:, cols] = qh.T
        gt[:, cols] = gh.T

    @pl.when(z < 4)
    def _():
        for j in range(NY):

            @pl.when(y <= j)
            def _(j=j):
                kv[12 + j] = jnp.zeros((2, TOK, D), BF16)

    for i in range(1, NH):
        head_arrival(i).wait_recv()

    def level_copy(level):
        src = kv.at[4 + y] if level == 3 else kv.at[OWN]
        slot = 4 * (level - 1) + y
        step = 1 if level == 3 else level
        return remote(src, kv.at[slot], kz_send.at[level - 1], kv_recv.at[slot], at_z(step))

    def level_goes(level):
        if level == 3:
            return (z >= 2) & (z < NZ - 1)
        return z < NZ - level

    def level_start(level):
        pl.when(level_goes(level))(lambda: level_copy(level).start())

    def spread_copy(level, i):
        src = kv.at[OWN] if level == 0 else kv.at[4 * (level - 1) + y]
        slot = 12 + y if level in (0, 4) else 4 * (level - 1) + y
        return remote(src, kv.at[slot], ky_send.at[3 * level + i - 1], kv_recv.at[slot], at_y(i))

    def spread_goes(level, i):
        if level == 0:
            return (y + i) < NY
        if level == 4:
            return (z >= 4) & ((y + i) >= NY)
        return z >= level

    def spread_start(level):
        for i in range(1, NY):

            @pl.when(spread_goes(level, i))
            def _(i=i):
                spread_copy(level, i).start()

    def slot_arrival(slot):
        remote(kv.at[slot], kv.at[slot], kz_send.at[0], kv_recv.at[slot], at_y(1)).wait_recv()

    for level in (1, 2, 4):
        level_start(level)
    spread_start(0)

    docs = doc_ref[...]
    mine = doc_ref[pl.ds(ctx, 1), :]
    starts = jnp.zeros((1, TOK), F32)
    for v in range(1, 4):
        below = jnp.where(docs < v, 1.0, 0.0).astype(F32)
        count = jnp.sum(jnp.sum(below, axis=0, keepdims=True), axis=1, keepdims=True)
        starts = jnp.where(mine == v, count, starts)
    starts = jnp.concatenate([starts, starts], axis=1)
    tpos = lax.broadcasted_iota(jnp.int32, (1, TOK), 1).astype(F32)
    tpos = jnp.concatenate([tpos, tpos], axis=1) + (ctx * TOK).astype(F32)

    def positions(bases):
        step = lax.broadcasted_iota(jnp.int32, (TOK, 1), 0).astype(F32)
        return jnp.concatenate([step + b.astype(F32) for b in bases], axis=0)

    def chunk_of(c):
        return slice(c * CHUNK, (c + 1) * CHUNK)

    def forward(group, slot0, count, bases, diagonal, halfway=None):
        n = count * TOK
        span = slice(slot0 * TOK, slot0 * TOK + n)
        keys = kv[slot0 : slot0 + count, 0].reshape(n, D)
        values = kv[slot0 : slot0 + count, 1].reshape(n, D)
        kt[:, span] = keys.T
        tr[:, :n] = values.T
        kpos = positions(bases)

        def step(c):
            cols = chunk_of(c)
            s = dot(keys, qt[:, cols]) * (SCALE * LOG2E)
            allowed = kpos >= starts
            if diagonal:
                allowed = allowed & (kpos <= tpos)
            s = jnp.where(allowed, s, NEG)
            top = jnp.max(s, axis=0, keepdims=True)
            if not diagonal:
                before = mrun[:, cols]
                top = jnp.maximum(before, top)
                fade = jnp.exp2(before - top)
            p = jnp.exp2(s - top)
            mass = jnp.sum(p, axis=0, keepdims=True)
            low = p.astype(BF16)
            pbuf[span, cols] = low
            part_o = dot(tr[:, :n], low)
            dpb[span, cols] = dot(values, gt[:, cols])
            if diagonal:
                lrun[:, cols] = mass
                ot[:, cols] = part_o
            else:
                lrun[:, cols] = lrun[:, cols] * fade + mass
                ot[:, cols] = ot[:, cols] * fade + part_o
            mrun[:, cols] = top
            mgrp[group : group + 1, cols] = top
            if halfway is not None and c == NCHUNK // 2 - 1:
                halfway()

        for c in range(NCHUNK):
            step(c)

    def level_bases(level):
        return [((z - level) * NY + j) * TOK for j in range(NY)]

    mix_bases = [jnp.where(j < y, z * NY + j, (z - 4) * NY + j) * TOK for j in range(NY)]

    def pass_on(level):
        @pl.when(z >= level)
        def _():
            slot_arrival(4 * (level - 1) + y)

        if level == 2:
            level_start(3)
        spread_start(level)

    def await_level(level):
        @pl.when(z >= level)
        def _():
            for i in range(1, NY):
                slot_arrival(4 * (level - 1) + (y + i) % NY)

    forward(0, OWN, 1, [ctx * TOK], True)
    pass_on(1)
    pass_on(2)
    await_level(1)
    pass_on(4)
    pl.when(z < 1)(lambda: pass_on(3))
    pl.when(z >= 1)(lambda: forward(1, 0, 4, level_bases(1), False, lambda: pass_on(3)))
    await_level(2)
    pl.when(z >= 2)(lambda: forward(2, 4, 4, level_bases(2), False))
    for i in range(1, NY):
        other = (y + i) % NY

        @pl.when((other < y) | (z >= 4))
        def _(other=other):
            slot_arrival(12 + other)

    forward(4, 12, 4, mix_bases, False)
    await_level(3)
    pl.when(z >= 3)(lambda: forward(3, 8, 4, level_bases(3), False))

    def finish(c):
        cols = chunk_of(c)
        mass = lrun[:, cols]
        out = (ot[:, cols] / mass).astype(BF16)
        wide = out.astype(F32)
        ot[:, cols] = wide
        delta[:, cols] = jnp.sum(gt[:, cols].astype(F32) * wide, axis=0, keepdims=True)

    for c in range(NCHUNK):
        finish(c)
    norm = mrun[...] * LN2 + jnp.log(lrun[...])
    for h in range(HG):
        cols = slice(h * D, (h + 1) * D)
        lown[h : h + 1, :] = norm[:, cols]
    reps = lax.broadcasted_iota(jnp.int32, (32, TOK), 1) // 4 == lax.broadcasted_iota(
        jnp.int32, (32, TOK), 0
    )
    owners = dot(owner_ref[pl.ds(ctx, 1), :].astype(F32), jnp.where(reps, 1.0, 0.0).astype(F32))
    to_col = lax.broadcasted_iota(jnp.int32, (TOK, TOK), 0)
    from_tok = lax.broadcasted_iota(jnp.int32, (TOK, TOK), 1)
    hit = (owners == (to_col // 4).astype(F32)) & (to_col % 4 == from_tok % 4)
    lgat[z, y] = lax.dot_general(
        lown[...],
        jnp.where(hit, 1.0, 0.0).astype(F32),
        (((1,), (1,)), ((), ())),
        precision=lax.Precision.HIGHEST,
        preferred_element_type=F32,
    )

    def lse_y(i):
        return remote(lgat.at[z, y], lgat.at[z, y], ly_send.at[i], ly_recv.at[i], at_y(i))

    def lse_y_arrival(i):
        other = (y + NY - i) % NY
        return remote(lgat.at[z, other], lgat.at[z, other], ly_send.at[i], ly_recv.at[i], at_y(i))

    def lse_up(step):
        block = lgat.at[(z + NZ - step) % NZ]
        return remote(block, block, lz_send.at[step], lz_recv.at[step], at_z(1))

    def lse_up_arrival(step):
        block = lgat.at[(z + NZ - 1 - step) % NZ]
        return remote(block, block, lz_send.at[step], lz_recv.at[step], at_z(1))

    def lse_down(step):
        block = lgat.at[(z + step) % NZ]
        return remote(block, block, lz_send.at[4 + step], lz_recv.at[4 + step], at_z(NZ - 1))

    def lse_down_arrival(step):
        block = lgat.at[(z + 1 + step) % NZ]
        return remote(block, block, lz_send.at[4 + step], lz_recv.at[4 + step], at_z(NZ - 1))

    def lse_step(step):
        if step == 0:
            for i in range(1, NY):
                lse_y_arrival(i).wait_recv()
        else:
            lse_up_arrival(step - 1).wait_recv()
            if step < 4:
                lse_down_arrival(step - 1).wait_recv()
        if step < 4:
            lse_up(step).start()
        if step < 3:
            lse_down(step).start()

    for i in range(1, NY):
        lse_y(i).start()

    def backward(group, slot0, count):
        n = count * TOK
        span = slice(slot0 * TOK, slot0 * TOK + n)

        def step(c):
            cols = chunk_of(c)
            share = jnp.exp2(mgrp[group : group + 1, cols] - mrun[:, cols]) / lrun[:, cols]
            p = pbuf[span, cols].astype(F32) * share
            dsb[span, cols] = (p * (dpb[span, cols] - delta[:, cols])).astype(BF16)
            pbuf[span, cols] = p.astype(BF16)

        for c in range(NCHUNK):
            step(c)
        part[slot0 : slot0 + count, 0] = dot(dsb[span, :], qs[...]).astype(BF16).reshape(count, TOK, D)
        part[slot0 : slot0 + count, 1] = dot(pbuf[span, :], gs[...]).astype(BF16).reshape(count, TOK, D)

    def query_gradient(slot0, count, first):
        span = slice(slot0 * TOK, (slot0 + count) * TOK)

        def step(c):
            cols = chunk_of(c)
            dq = dot(kt[:, span], dsb[span, cols])
            if first:
                dqt[:, cols] = dq
            else:
                dqt[:, cols] += dq

        for c in range(NCHUNK):
            step(c)

    def grad_y(g, i):
        other = (y + i) % NY
        return remote(
            part.at[4 * g + other], yrecv.at[g, y], gy_send.at[3 * g + i - 1],
            gy_recv.at[4 * g + y], at_y(i),
        )

    def grad_y_goes(g, i, part_of=None):
        if g < 3:
            return z >= g + 1
        own_level, far_level = (y + i) >= NY, ((y + i) < NY) & (z >= 4)
        return {None: own_level | far_level, 0: own_level, 4: far_level}[part_of]

    def grad_y_start(g, part_of=None):
        for i in range(1, NY):

            @pl.when(grad_y_goes(g, i, part_of))
            def _(i=i):
                grad_y(g, i).start()

    def grad_y_arrival(g, other):
        remote(
            yrecv.at[g, other], yrecv.at[g, other], gy_send.at[0], gy_recv.at[4 * g + other], at_y(1)
        ).wait_recv()

    def wide(ref, *at):
        return ref[at].astype(F32)

    def grad_z(level):
        to = (jnp.maximum(z - (1 if level == 3 else 2), 0) * NY + y, head)
        at = level - 2
        return remote(zsend.at[at], zrecv.at[at], gz_send.at[at], gz_recv.at[at], to)

    def column_sum(level):
        g = level - 1
        total[...] = wide(part, 4 * g + y)
        for i in range(1, NY):
            other = (y + i) % NY
            if level == 4:

                @pl.when(other < y)
                def _(other=other):
                    grad_y_arrival(g, other)
                    total[...] += wide(yrecv, g, other)
            else:
                grad_y_arrival(g, other)
                total[...] += wide(yrecv, g, other)

    def from_z(level):
        grad_z(level).wait_recv()
        total[...] += wide(zrecv, level - 2)

    def reduce_level(level):
        @pl.when(z >= level)
        def _():
            column_sum(level)
            if level == 2:
                pl.when(z < NZ - 2)(lambda: from_z(4))
                pl.when(z < NZ - 1)(lambda: from_z(3))
            zsend[level - 2] = total[...].astype(BF16)
            grad_z(level).start()

    def home_rows(to):
        return pl.ds(pl.multiple_of(to * TOKDEV, TOKDEV), TOKDEV)

    def home(i):
        return remote(
            pieces.at[0, :, home_rows((head + i) % NH), :], hrecv.at[0, head],
            hb_send.at[0, i], hb_recv.at[0, i], at_head(i),
        )

    def home_arrival(i):
        ref = hrecv.at[0, (head + NH - i) % NH]
        return remote(ref, ref, hb_send.at[0, i], hb_recv.at[0, i], at_head(i))

    def home_down(i):
        to = (head + i) % NH
        return remote(
            pieces.at[1, :, home_rows(to), :], hrecv.at[1, head],
            hb_send.at[1, i], hb_recv.at[1, i], (jnp.maximum(z - 1, 0) * NY + y, to),
        )

    def home_down_arrival(i):
        ref = hrecv.at[1, (head + NH - i) % NH]
        return remote(ref, ref, hb_send.at[1, i], hb_recv.at[1, i], at_head(i))

    def leave(at):
        pieces[at, 0] = (total[0] * SCALE).astype(BF16)
        pieces[at, 1] = total[1].astype(BF16)

    def at_level(level, fn, *args):
        pl.when(z >= level)(lambda: fn(*args))

    backward(4, 12, 4)
    grad_y_start(3, 4)
    at_level(3, backward, 3, 8, 4)
    grad_y_start(2)
    at_level(2, backward, 2, 4, 4)
    grad_y_start(1)
    at_level(1, backward, 1, 0, 4)
    grad_y_start(0)
    grad_y_start(3, 0)
    lse_step(0)
    reduce_level(4)
    backward(0, OWN, 1)
    query_gradient(OWN, 1, True)
    query_gradient(12, 4, False)
    reduce_level(3)
    lse_step(1)
    at_level(3, query_gradient, 8, 4, False)
    for h in range(HG):
        cols = slice(h * D, (h + 1) * D)
        att_ref[:, cols] = ot[:, cols].T.astype(BF16)
    stores[0].start()
    at_level(2, query_gradient, 4, 4, False)
    at_level(1, query_gradient, 0, 4, False)
    reduce_level(2)
    lse_step(2)
    for h in range(HG):
        cols = slice(h * D, (h + 1) * D)
        gq_ref[:, cols] = (dqt[:, cols] * SCALE).T.astype(BF16)
    stores[1].start()

    @pl.when(z >= 1)
    def _():
        column_sum(1)
        leave(1)
        for i in range(NH):
            home_down(i).start()

    lse_step(3)
    total[...] = wide(part, OWN)
    for i in range(1, NY):
        other = (y + i) % NY

        @pl.when(other > y)
        def _(other=other):
            grad_y_arrival(3, other)
            total[...] += wide(yrecv, 3, other)

    pl.when(z < NZ - 2)(lambda: from_z(2))
    leave(0)
    for i in range(1, NH):
        home(i).start()
    hrecv[0, head] = pieces[0, :, home_rows(head), :]

    lse_step(4)
    lane = lax.broadcasted_iota(jnp.int32, (HG, TOK), 1) // 4
    owned = jnp.zeros((HG, TOK), F32)
    for d in range(NZ * NY):
        moved = pltpu.roll(lgat[d // NY, d % NY], ((d - ctx) * 4) % TOK, 1)
        owned = jnp.where(lane == d, moved, owned)
    lse_ref[...] = owned
    stores[2].start()

    for i in range(1, NH):
        head_copy(i).wait_send()
    for hop in range(1, 5):

        @pl.when(level_goes(hop))
        def _(hop=hop):
            level_copy(hop).wait_send()

        if hop > 1:

            @pl.when(z >= hop)
            def _(hop=hop):
                grad_z(hop).wait_send()

    for level in range(5):
        for i in range(1, NY):

            @pl.when(spread_goes(level, i))
            def _(level=level, i=i):
                spread_copy(level, i).wait_send()

    for g in range(4):
        for i in range(1, NY):

            @pl.when(grad_y_goes(g, i))
            def _(g=g, i=i):
                grad_y(g, i).wait_send()

    for i in range(1, NY):
        lse_y(i).wait_send()
    for step in range(4):
        lse_up(step).wait_send()
    for step in range(3):
        lse_down(step).wait_send()

    @pl.when(z == NZ - 1)
    def _():
        hrecv[1] = jnp.zeros((NH, 2, TOKDEV, D), BF16)

    @pl.when(z < NZ - 1)
    def _():
        for i in range(NH):
            home_down_arrival(i).wait_recv()

    for i in range(1, NH):
        home_arrival(i).wait_recv()
    for h in range(NH):
        cols = slice(h * D, (h + 1) * D)
        both = wide(hrecv, 0, h) + wide(hrecv, 1, h)
        gk_ref[:, cols] = both[0].astype(BF16)
        gv_ref[:, cols] = both[1].astype(BF16)
    stores[3].start()
    stores[4].start()

    @pl.when(z >= 1)
    def _():
        for i in range(NH):
            home_down(i).wait_send()

    for i in range(1, NH):
        home(i).wait_send()
    for store in stores:
        store.wait()


def deliver(*refs):
    sem = refs[-1]
    copies = [pltpu.make_async_copy(refs[i], refs[5 + i], sem.at[i]) for i in range(5)]
    for copy in copies:
        copy.start()
    for copy in copies:
        copy.wait()


def body(queries, key_rows, value_rows, grad_out, doc_ids, block_owner):
    hbm = pl.BlockSpec(memory_space=pltpu.HBM)
    dma = pltpu.SemaphoreType.DMA
    keys = 17 * TOK
    shapes = (
        jax.ShapeDtypeStruct((TOK, ROWS), BF16),
        jax.ShapeDtypeStruct((HG, TOK), F32),
        jax.ShapeDtypeStruct((TOK, ROWS), BF16),
        jax.ShapeDtypeStruct((TOKDEV, NH * D), BF16),
        jax.ShapeDtypeStruct((TOKDEV, NH * D), BF16),
    )
    outs = pl.pallas_call(
        kernel,
        out_shape=shapes,
        in_specs=[hbm] * 6,
        out_specs=(hbm,) * 5,
        scratch_shapes=[
            pltpu.VMEM((TOK, ROWS), BF16),
            pltpu.VMEM((TOK, ROWS), BF16),
            pltpu.VMEM((TOKDEV, NH * D), BF16),
            pltpu.VMEM((TOKDEV, NH * D), BF16),
            pltpu.VMEM((32, TOK), jnp.int32),
            pltpu.VMEM((32, 32), jnp.int32),
            pltpu.VMEM((TOK, ROWS), BF16),
            pltpu.VMEM((HG, TOK), F32),
            pltpu.VMEM((TOK, ROWS), BF16),
            pltpu.VMEM((TOKDEV, NH * D), BF16),
            pltpu.VMEM((TOKDEV, NH * D), BF16),
            dma((5,)),
            pltpu.VMEM((D, ROWS), BF16),
            pltpu.VMEM((D, ROWS), BF16),
            pltpu.VMEM((ROWS, D), BF16),
            pltpu.VMEM((ROWS, D), BF16),
            pltpu.VMEM((17, 2, TOK, D), BF16),
            pltpu.VMEM((NH, 2, TOKDEV, D), BF16),
            pltpu.VMEM((keys, ROWS), BF16),
            pltpu.VMEM((keys, ROWS), F32),
            pltpu.VMEM((keys, ROWS), BF16),
            pltpu.VMEM((D, keys), BF16),
            pltpu.VMEM((D, 4 * TOK), BF16),
            pltpu.VMEM((D, ROWS), F32),
            pltpu.VMEM((D, ROWS), F32),
            pltpu.VMEM((1, ROWS), F32),
            pltpu.VMEM((1, ROWS), F32),
            pltpu.VMEM((8, ROWS), F32),
            pltpu.VMEM((1, ROWS), F32),
            pltpu.VMEM((17, 2, TOK, D), BF16),
            pltpu.VMEM((4, NY, 2, TOK, D), BF16),
            pltpu.VMEM((3, 2, TOK, D), BF16),
            pltpu.VMEM((3, 2, TOK, D), BF16),
            pltpu.VMEM((2, TOK, D), F32),
            pltpu.VMEM((2, 2, TOK, D), BF16),
            pltpu.VMEM((2, NH, 2, TOKDEV, D), BF16),
            pltpu.VMEM((HG, TOK), F32),
            pltpu.VMEM((NZ, NY, HG, TOK), F32),
            dma((6,)),
            dma((NH,)), dma((NH,)),
            dma((4,)), dma((15,)), dma((17,)),
            dma((12,)), dma((16,)), dma((3,)), dma((3,)),
            dma((2, NH)), dma((2, NH)),
            dma((NY,)), dma((NY,)), dma((NZ,)), dma((NZ,)),
        ],
        compiler_params=pltpu.CompilerParams(
            collective_id=0, has_side_effects=True, vmem_limit_bytes=60 * 1024 * 1024
        ),
        name="packed_attention",
    )(queries, key_rows, value_rows, grad_out, doc_ids.reshape(32, TOK), block_owner)
    return pl.pallas_call(
        deliver,
        out_shape=shapes,
        in_specs=[pl.BlockSpec(memory_space=pltpu.VMEM)] * 5,
        out_specs=(hbm,) * 5,
        scratch_shapes=[dma((5,))],
        name="deliver",
    )(*outs)


def solution(mesh):
    return jax.shard_map(
        body,
        mesh=mesh,
        in_specs=(
            P("ctx", "head"), P(("ctx", "head"), None), P(("ctx", "head"), None),
            P("ctx", "head"), P(), P(),
        ),
        out_specs=(
            P("ctx", "head"), P("head", "ctx"), P("ctx", "head"),
            P(("ctx", "head"), None), P(("ctx", "head"), None),
        ),
        check_vma=False,
    )
```

```python
import jax
import jax.numpy as jnp
from jax import lax
from jax.experimental import pallas as pl
from jax.experimental.pallas import tpu as pltpu
from jax.sharding import PartitionSpec as P

D = 128
TOK = 128
HG = 8
ROWS = HG * TOK
CHUNK = 256
NCHUNK = ROWS // CHUNK
NZ, NY = 8, 4
NH = 8
TOKDEV = 16
OWN = 16
LOG2E = 1.4426950408889634
LN2 = 0.6931471805599453
NEG = -1e30
SCALE = D**-0.5
F32 = jnp.float32
BF16 = jnp.bfloat16
MESH = pl.DeviceIdType.MESH


def dot(a, b):
    return jnp.dot(a, b, preferred_element_type=F32)


def kernel(
    q_hbm, k_hbm, v_hbm, g_hbm, doc_hbm, owner_hbm,
    att_ref, lse_ref, gq_ref, gk_ref, gv_ref,
    q_in, g_in, k_ref, v_ref, doc_ref, owner_ref,
    qt, gt, qs, gs, kv, stage, pbuf, dpb, dsb, ot, dqt, mrun, lrun, mgrp, delta,
    part, yrecv, total, pieces, hrecv, gathered, lown, lgat,
    load_sem, ha_send, ha_recv, kz_send, ky_send, kv_recv,
    gy_send, gy_recv, hb_send, hb_recv, ly_send, ly_recv, lz_send, lz_recv,
):
    ctx = lax.axis_index("ctx")
    head = lax.axis_index("head")
    z = ctx // NY
    y = ctx % NY

    loads = [
        pltpu.make_async_copy(src, dst, load_sem.at[i])
        for i, (src, dst) in enumerate(
            (
                (k_hbm, k_ref), (v_hbm, v_ref), (q_hbm, q_in), (g_hbm, g_in),
                (doc_hbm, doc_ref), (owner_hbm, owner_ref),
            )
        )
    ]
    for load in loads:
        load.start()

    def at_head(i):
        return (ctx, (head + i) % NH)

    def at_y(i):
        return (z * NY + (y + i) % NY, head)

    def at_z(i):
        return (((z + i) % NZ) * NY + y, head)

    barrier = pltpu.get_barrier_semaphore()
    for i in range(1, NH):
        pl.semaphore_signal(barrier, inc=1, device_id=at_head(i), device_id_type=MESH)
    for i in range(1, NY):
        pl.semaphore_signal(barrier, inc=1, device_id=at_y(i), device_id_type=MESH)
    for i in (1, 2, 4):

        @pl.when(z >= i)
        def _(i=i):
            pl.semaphore_signal(barrier, inc=1, device_id=at_z(NZ - i), device_id_type=MESH)


    for i in (5, 6, 7):

        @pl.when(z < NZ - i)
        def _(i=i):
            pl.semaphore_signal(barrier, inc=1, device_id=at_z(i), device_id_type=MESH)

    loads[0].wait()
    loads[1].wait()
    for h in range(NH):
        stage[h, 0] = k_ref[:, h * D : (h + 1) * D]
        stage[h, 1] = v_ref[:, h * D : (h + 1) * D]
    above = sum((z < NZ - i).astype(jnp.int32) for i in (1, 2, 4))
    below = sum((z >= i).astype(jnp.int32) for i in (5, 6, 7))
    pl.semaphore_wait(barrier, NH + NY - 2 + above + below)

    def remote(src, dst, ssem, rsem, to):
        return pltpu.make_async_remote_copy(
            src_ref=src, dst_ref=dst, send_sem=ssem, recv_sem=rsem, device_id=to, device_id_type=MESH
        )

    def head_copy(i):
        to = (head + i) % NH
        rows = pl.ds(pl.multiple_of(head * TOKDEV, TOKDEV), TOKDEV)
        return remote(
            stage.at[to], kv.at[OWN, :, rows, :], ha_send.at[i], ha_recv.at[i], at_head(i)
        )

    def head_arrival(i):
        rows = pl.ds(pl.multiple_of(((head + NH - i) % NH) * TOKDEV, TOKDEV), TOKDEV)
        return remote(stage.at[0], kv.at[OWN, :, rows, :], ha_send.at[i], ha_recv.at[i], at_head(i))

    for i in range(1, NH):
        head_copy(i).start()
    kv[OWN, :, pl.ds(pl.multiple_of(head * TOKDEV, TOKDEV), TOKDEV), :] = stage[head]

    for load in loads[2:]:
        load.wait()
    for h in range(HG):
        cols = slice(h * D, (h + 1) * D)
        qh, gh = q_in[:, cols], g_in[:, cols]
        qs[cols, :] = qh
        gs[cols, :] = gh
        qt[:, cols] = qh.T
        gt[:, cols] = gh.T

    @pl.when(z < 4)
    def _():
        for j in range(NY):

            @pl.when(y <= j)
            def _(j=j):
                kv[12 + j] = jnp.zeros((2, TOK, D), BF16)

    for i in range(1, NH):
        head_arrival(i).wait_recv()

    def level_copy(level, half):
        src = kv.at[4 + y, half] if level == 3 else kv.at[OWN, half]
        slot = 4 * (level - 1) + y
        step = 1 if level == 3 else level
        return remote(
            src, kv.at[slot, half], kz_send.at[half, level - 1], kv_recv.at[half, slot], at_z(step)
        )

    def level_goes(level):
        if level == 3:
            return (z >= 2) & (z < NZ - 1)
        return z < NZ - level

    def level_start(level, half):
        pl.when(level_goes(level))(lambda: level_copy(level, half).start())

    def spread_copy(level, half, i):
        src = kv.at[OWN, half] if level == 0 else kv.at[4 * (level - 1) + y, half]
        slot = 12 + y if level in (0, 4) else 4 * (level - 1) + y
        return remote(
            src, kv.at[slot, half], ky_send.at[half, 3 * level + i - 1], kv_recv.at[half, slot], at_y(i)
        )

    def spread_goes(level, i):
        if level == 0:
            return (y + i) < NY
        if level == 4:
            return (z >= 4) & ((y + i) >= NY)
        return z >= level

    def spread_start(level, half):
        for i in range(1, NY):
            pl.when(spread_goes(level, i))(lambda i=i: spread_copy(level, half, i).start())

    def slot_arrival(slot, half):
        ref = kv.at[slot, half]
        remote(ref, ref, kz_send.at[0, 0], kv_recv.at[half, slot], at_y(1)).wait_recv()

    for half in range(2):
        for level in (1, 2, 4):
            level_start(level, half)
        spread_start(0, half)

    docs = doc_ref[...]
    mine = doc_ref[pl.ds(ctx, 1), :]
    starts = jnp.zeros((1, TOK), F32)
    for v in range(1, 4):
        below = jnp.where(docs < v, 1.0, 0.0).astype(F32)
        count = jnp.sum(jnp.sum(below, axis=0, keepdims=True), axis=1, keepdims=True)
        starts = jnp.where(mine == v, count, starts)
    starts = jnp.concatenate([starts, starts], axis=1)
    tpos = lax.broadcasted_iota(jnp.int32, (1, TOK), 1).astype(F32)
    tpos = jnp.concatenate([tpos, tpos], axis=1) + (ctx * TOK).astype(F32)

    def positions(bases):
        step = lax.broadcasted_iota(jnp.int32, (TOK, 1), 0).astype(F32)
        return jnp.concatenate([step + b.astype(F32) for b in bases], axis=0)

    def chunk_of(c):
        return slice(c * CHUNK, (c + 1) * CHUNK)

    def score(group, slot0, count, bases, diagonal=False):
        n = count * TOK
        span = slice(slot0 * TOK, slot0 * TOK + n)
        keys = kv[slot0 : slot0 + count, 0].reshape(n, D)
        kpos = positions(bases)

        def step(c):
            cols = chunk_of(c)
            s = dot(keys, qt[:, cols]) * (SCALE * LOG2E)
            allowed = kpos >= starts
            if diagonal:
                allowed = allowed & (kpos <= tpos)
            s = jnp.where(allowed, s, NEG)
            top = jnp.max(s, axis=0, keepdims=True)
            if not diagonal:
                before = mrun[:, cols]
                top = jnp.maximum(before, top)
            p = jnp.exp2(s - top)
            mass = jnp.sum(p, axis=0, keepdims=True)
            if not diagonal:
                mass += lrun[:, cols] * jnp.exp2(before - top)
            pbuf[span, cols] = p.astype(BF16)
            lrun[:, cols] = mass
            mrun[:, cols] = top
            mgrp[group : group + 1, cols] = top

        for c in range(NCHUNK):
            step(c)

    def normalise(group, slot0, count):
        span = slice(slot0 * TOK, (slot0 + count) * TOK)

        def step(c):
            cols = chunk_of(c)
            share = jnp.exp2(mgrp[group : group + 1, cols] - mrun[:, cols]) / lrun[:, cols]
            pbuf[span, cols] = (pbuf[span, cols].astype(F32) * share).astype(BF16)

        for c in range(NCHUNK):
            step(c)
        part[slot0 : slot0 + count, 1] = dot(pbuf[span, :], gs[...]).astype(BF16).reshape(count, TOK, D)

    def with_values(slot0, count, first=False):
        n = count * TOK
        span = slice(slot0 * TOK, slot0 * TOK + n)
        values = kv[slot0 : slot0 + count, 1].reshape(n, D)
        across = values.T

        def step(c):
            cols = chunk_of(c)
            dpb[span, cols] = dot(values, gt[:, cols])
            part_o = dot(across, pbuf[span, cols])
            if first:
                ot[:, cols] = part_o
            else:
                ot[:, cols] += part_o

        for c in range(NCHUNK):
            step(c)

    def level_bases(level):
        return [((z - level) * NY + j) * TOK for j in range(NY)]

    mix_bases = [jnp.where(j < y, z * NY + j, (z - 4) * NY + j) * TOK for j in range(NY)]

    def pass_on(level, half):
        pl.when(z >= level)(lambda: slot_arrival(4 * (level - 1) + y, half))
        if level == 2:
            level_start(3, half)
        spread_start(level, half)

    def await_level(level, half):
        @pl.when(z >= level)
        def _():
            for i in range(1, NY):
                slot_arrival(4 * (level - 1) + (y + i) % NY, half)

    def await_mix(half):
        for i in range(1, NY):
            other = (y + i) % NY
            pl.when((other < y) | (z >= 4))(lambda other=other: slot_arrival(12 + other, half))

    def at_level(level, fn, *args):
        pl.when(z >= level)(lambda: fn(*args))

    score(0, OWN, 1, [ctx * TOK], True)
    pass_on(1, 0)
    pass_on(2, 0)
    pass_on(4, 0)
    pass_on(1, 1)
    await_level(1, 0)
    at_level(1, score, 1, 0, 4, level_bases(1))
    pass_on(3, 0)
    pass_on(2, 1)
    await_level(2, 0)
    at_level(2, score, 2, 4, 4, level_bases(2))
    pass_on(4, 1)
    await_mix(0)
    score(4, 12, 4, mix_bases)
    pass_on(3, 1)
    await_level(3, 0)
    at_level(3, score, 3, 8, 4, level_bases(3))

    def grad_y(g, half, i):
        other = (y + i) % NY
        return remote(
            part.at[4 * g + other, half], yrecv.at[g, y, half], gy_send.at[half, 3 * g + i - 1],
            gy_recv.at[half, 4 * g + y], at_y(i),
        )

    def grad_y_goes(g, i, part_of=None):
        if g < 3:
            return z >= g + 1
        own_level, far_level = (y + i) >= NY, ((y + i) < NY) & (z >= 4)
        return {None: own_level | far_level, 0: own_level, 4: far_level}[part_of]

    def grad_y_start(g, half, part_of=None):
        for i in range(1, NY):
            pl.when(grad_y_goes(g, i, part_of))(lambda i=i: grad_y(g, half, i).start())

    def grad_y_arrival(g, other):
        for half in range(2):
            ref = yrecv.at[g, other, half]
            remote(ref, ref, gy_send.at[0, 0], gy_recv.at[half, 4 * g + other], at_y(1)).wait_recv()

    normalise(4, 12, 4)
    grad_y_start(3, 1, 4)
    at_level(3, normalise, 3, 8, 4)
    grad_y_start(2, 1)
    at_level(2, normalise, 2, 4, 4)
    grad_y_start(1, 1)
    at_level(1, normalise, 1, 0, 4)
    grad_y_start(0, 1)
    grad_y_start(3, 1, 0)
    normalise(0, OWN, 1)

    norm = mrun[...] * LN2 + jnp.log(lrun[...])
    for h in range(HG):
        cols = slice(h * D, (h + 1) * D)
        lown[h : h + 1, :] = norm[:, cols]
    reps = lax.broadcasted_iota(jnp.int32, (32, TOK), 1) // 4 == lax.broadcasted_iota(
        jnp.int32, (32, TOK), 0
    )
    owners = dot(owner_ref[pl.ds(ctx, 1), :].astype(F32), jnp.where(reps, 1.0, 0.0).astype(F32))
    to_col = lax.broadcasted_iota(jnp.int32, (TOK, TOK), 0)
    from_tok = lax.broadcasted_iota(jnp.int32, (TOK, TOK), 1)
    hit = (owners == (to_col // 4).astype(F32)) & (to_col % 4 == from_tok % 4)
    lgat[z, y] = lax.dot_general(
        lown[...],
        jnp.where(hit, 1.0, 0.0).astype(F32),
        (((1,), (1,)), ((), ())),
        precision=lax.Precision.HIGHEST,
        preferred_element_type=F32,
    )

    def lse_y(i):
        return remote(lgat.at[z, y], lgat.at[z, y], ly_send.at[i], ly_recv.at[i], at_y(i))

    def lse_y_arrival(i):
        other = (y + NY - i) % NY
        return remote(lgat.at[z, other], lgat.at[z, other], ly_send.at[i], ly_recv.at[i], at_y(i))

    def lse_z(i):
        return remote(lgat.at[z], lgat.at[z], lz_send.at[i], lz_recv.at[i], at_z(i))

    def lse_z_arrival(i):
        block = lgat.at[(z + NZ - i) % NZ]
        return remote(block, block, lz_send.at[i], lz_recv.at[i], at_z(i))

    def lse_down():
        for i in range(1, NY):
            lse_y_arrival(i).wait_recv()
        for i in range(1, NZ):
            pl.when(z >= NZ - i)(lambda i=i: lse_z(i).start())

    def lse_up():
        for i in range(1, NZ):

            @pl.when(z < NZ - i)
            def _(i=i):
                lse_z_arrival(NZ - i).wait_recv()
                lse_z(i).start()

    for i in range(1, NY):
        lse_y(i).start()

    with_values(OWN, 1, True)
    await_level(1, 1)
    at_level(1, with_values, 0, 4)
    await_level(2, 1)
    at_level(2, with_values, 4, 4)
    await_mix(1)
    with_values(12, 4)
    await_level(3, 1)
    at_level(3, with_values, 8, 4)

    def finish(c):
        cols = chunk_of(c)
        full = ot[:, cols].astype(BF16).astype(F32)
        ot[:, cols] = full
        delta[:, cols] = jnp.sum(gt[:, cols].astype(F32) * full, axis=0, keepdims=True)

    for c in range(NCHUNK):
        finish(c)

    def backward(slot0, count):
        span = slice(slot0 * TOK, (slot0 + count) * TOK)

        def step(c):
            cols = chunk_of(c)
            slope = dpb[span, cols] - delta[:, cols]
            dsb[span, cols] = (pbuf[span, cols].astype(F32) * slope).astype(BF16)

        for c in range(NCHUNK):
            step(c)
        part[slot0 : slot0 + count, 0] = dot(dsb[span, :], qs[...]).astype(BF16).reshape(count, TOK, D)

    def query_gradient(slot0, count, first):
        span = slice(slot0 * TOK, (slot0 + count) * TOK)
        across = kv[slot0 : slot0 + count, 0].reshape(count * TOK, D).T

        def step(c):
            cols = chunk_of(c)
            dq = dot(across, dsb[span, cols])
            if first:
                dqt[:, cols] = dq
            else:
                dqt[:, cols] += dq

        for c in range(NCHUNK):
            step(c)

    def wide(ref, *at):
        return ref[at].astype(F32)

    def column_sum(level):
        g = level - 1
        total[...] = wide(part, 4 * g + y)
        for i in range(1, NY):
            other = (y + i) % NY
            if level == 4:

                @pl.when(other < y)
                def _(other=other):
                    grad_y_arrival(g, other)
                    total[...] += wide(yrecv, g, other)
            else:
                grad_y_arrival(g, other)
                total[...] += wide(yrecv, g, other)

    def home_rows(to):
        return pl.ds(pl.multiple_of(to * TOKDEV, TOKDEV), TOKDEV)

    def home(level, i):
        to = (head + i) % NH
        return remote(
            pieces.at[level, :, home_rows(to), :], hrecv.at[level, head],
            hb_send.at[level, i], hb_recv.at[level, i], (jnp.maximum(z - level, 0) * NY + y, to),
        )

    def home_arrival(level, i):
        ref = hrecv.at[level, (head + NH - i) % NH]
        return remote(ref, ref, hb_send.at[level, i], hb_recv.at[level, i], at_head(1))

    def home_start(level):
        pieces[level, 0] = (total[0] * SCALE).astype(BF16)
        pieces[level, 1] = total[1].astype(BF16)
        for i in range(0 if level else 1, NH):
            home(level, i).start()

    def reduce_level(level):
        @pl.when(z >= level)
        def _():
            column_sum(level)
            home_start(level)

    backward(12, 4)
    grad_y_start(3, 0, 4)
    at_level(3, backward, 8, 4)
    grad_y_start(2, 0)
    at_level(2, backward, 4, 4)
    grad_y_start(1, 0)
    at_level(1, backward, 0, 4)
    grad_y_start(0, 0)
    grad_y_start(3, 0, 0)
    lse_down()
    reduce_level(4)
    backward(OWN, 1)
    query_gradient(OWN, 1, True)
    query_gradient(12, 4, False)
    reduce_level(3)
    at_level(3, query_gradient, 8, 4, False)
    for h in range(HG):
        cols = slice(h * D, (h + 1) * D)
        att_ref[:, cols] = ot[:, cols].T.astype(BF16)
    at_level(2, query_gradient, 4, 4, False)
    at_level(1, query_gradient, 0, 4, False)
    reduce_level(2)
    for h in range(HG):
        cols = slice(h * D, (h + 1) * D)
        gq_ref[:, cols] = (dqt[:, cols] * SCALE).T.astype(BF16)

    reduce_level(1)
    lse_up()
    total[...] = wide(part, OWN)
    for i in range(1, NY):
        other = (y + i) % NY

        @pl.when(other > y)
        def _(other=other):
            grad_y_arrival(3, other)
            total[...] += wide(yrecv, 3, other)

    home_start(0)
    hrecv[0, head] = pieces[0, :, home_rows(head), :]

    for i in range(1, NZ):
        pl.when(z >= i)(lambda i=i: lse_z_arrival(i).wait_recv())
    lane = lax.broadcasted_iota(jnp.int32, (HG, TOK), 1) // 4
    owned = jnp.zeros((HG, TOK), F32)
    for d in range(NZ * NY):
        moved = pltpu.roll(lgat[d // NY, d % NY], ((d - ctx) * 4) % TOK, 1)
        owned = jnp.where(lane == d, moved, owned)
    lse_ref[...] = owned

    for i in range(1, NH):
        head_copy(i).wait_send()
    for hop in range(1, 5):

        @pl.when(level_goes(hop))
        def _(hop=hop):
            for half in range(2):
                level_copy(hop, half).wait_send()

    for level in range(5):
        for i in range(1, NY):

            @pl.when(spread_goes(level, i))
            def _(level=level, i=i):
                for half in range(2):
                    spread_copy(level, half, i).wait_send()

    for g in range(4):
        for i in range(1, NY):

            @pl.when(grad_y_goes(g, i))
            def _(g=g, i=i):
                for half in range(2):
                    grad_y(g, half, i).wait_send()

    for i in range(1, NY):
        lse_y(i).wait_send()
    for i in range(1, NZ):
        lse_z(i).wait_send()

    for i in range(1, NH):
        home_arrival(0, i).wait_recv()
    gathered[...] = wide(hrecv, 0)
    for level in range(1, 5):

        @pl.when(z < NZ - level)
        def _(level=level):
            for i in range(NH):
                home_arrival(level, i).wait_recv()
            gathered[...] += wide(hrecv, level)

    for h in range(NH):
        cols = slice(h * D, (h + 1) * D)
        gk_ref[:, cols] = gathered[h, 0].astype(BF16)
        gv_ref[:, cols] = gathered[h, 1].astype(BF16)

    for level in range(1, 5):

        @pl.when(z >= level)
        def _(level=level):
            for i in range(NH):
                home(level, i).wait_send()

    for i in range(1, NH):
        home(0, i).wait_send()


def deliver(*refs):
    sem = refs[-1]
    copies = [pltpu.make_async_copy(refs[i], refs[5 + i], sem.at[i]) for i in range(5)]
    for copy in copies:
        copy.start()
    for copy in copies:
        copy.wait()


def body(queries, key_rows, value_rows, grad_out, doc_ids, block_owner):
    hbm = pl.BlockSpec(memory_space=pltpu.HBM)
    dma = pltpu.SemaphoreType.DMA
    keys = 17 * TOK
    shapes = (
        jax.ShapeDtypeStruct((TOK, ROWS), BF16),
        jax.ShapeDtypeStruct((HG, TOK), F32),
        jax.ShapeDtypeStruct((TOK, ROWS), BF16),
        jax.ShapeDtypeStruct((TOKDEV, NH * D), BF16),
        jax.ShapeDtypeStruct((TOKDEV, NH * D), BF16),
    )
    arrays = (queries, key_rows, value_rows, grad_out, doc_ids.reshape(32, TOK), block_owner)
    outs = pl.pallas_call(
        kernel,
        out_shape=shapes,
        in_specs=[hbm] * 6,
        out_specs=(pl.BlockSpec(memory_space=pltpu.VMEM),) * 5,
        scratch_shapes=[
            pltpu.VMEM((TOK, ROWS), BF16),
            pltpu.VMEM((TOK, ROWS), BF16),
            pltpu.VMEM((TOKDEV, NH * D), BF16),
            pltpu.VMEM((TOKDEV, NH * D), BF16),
            pltpu.VMEM((32, TOK), jnp.int32),
            pltpu.VMEM((32, 32), jnp.int32),
            pltpu.VMEM((D, ROWS), BF16),
            pltpu.VMEM((D, ROWS), BF16),
            pltpu.VMEM((ROWS, D), BF16),
            pltpu.VMEM((ROWS, D), BF16),
            pltpu.VMEM((17, 2, TOK, D), BF16),
            pltpu.VMEM((NH, 2, TOKDEV, D), BF16),
            pltpu.VMEM((keys, ROWS), BF16),
            pltpu.VMEM((keys, ROWS), F32),
            pltpu.VMEM((keys, ROWS), BF16),
            pltpu.VMEM((D, ROWS), F32),
            pltpu.VMEM((D, ROWS), F32),
            pltpu.VMEM((1, ROWS), F32),
            pltpu.VMEM((1, ROWS), F32),
            pltpu.VMEM((8, ROWS), F32),
            pltpu.VMEM((1, ROWS), F32),
            pltpu.VMEM((17, 2, TOK, D), BF16),
            pltpu.VMEM((4, NY, 2, TOK, D), BF16),
            pltpu.VMEM((2, TOK, D), F32),
            pltpu.VMEM((5, 2, TOK, D), BF16),
            pltpu.VMEM((5, NH, 2, TOKDEV, D), BF16),
            pltpu.VMEM((NH, 2, TOKDEV, D), F32),
            pltpu.VMEM((HG, TOK), F32),
            pltpu.VMEM((NZ, NY, HG, TOK), F32),
            dma((6,)),
            dma((NH,)), dma((NH,)),
            dma((2, 4)), dma((2, 15)), dma((2, 17)),
            dma((2, 12)), dma((2, 16)),
            dma((5, NH)), dma((5, NH)),
            dma((NY,)), dma((NY,)), dma((NZ,)), dma((NZ,)),
        ],
        compiler_params=pltpu.CompilerParams(
            collective_id=0, has_side_effects=True, vmem_limit_bytes=48 * 1024 * 1024
        ),
        name="packed_attention",
    )(*(pltpu.with_memory_space_constraint(a, pltpu.HBM) for a in arrays))
    return pl.pallas_call(
        deliver,
        out_shape=shapes,
        in_specs=[pl.BlockSpec(memory_space=pltpu.VMEM)] * 5,
        out_specs=(hbm,) * 5,
        scratch_shapes=[dma((5,))],
        compiler_params=pltpu.CompilerParams(vmem_limit_bytes=2 * 1024 * 1024),
        name="deliver",
    )(*outs)


def solution(mesh):
    return jax.shard_map(
        body,
        mesh=mesh,
        in_specs=(
            P("ctx", "head"), P(("ctx", "head"), None), P(("ctx", "head"), None),
            P("ctx", "head"), P(), P(),
        ),
        out_specs=(
            P("ctx", "head"), P("head", "ctx"), P("ctx", "head"),
            P(("ctx", "head"), None), P(("ctx", "head"), None),
        ),
        check_vma=False,
    )
```

```python
import jax
import jax.numpy as jnp
from jax import lax
from jax.experimental import pallas as pl
from jax.experimental.pallas import tpu as pltpu
from jax.sharding import PartitionSpec as P

D = 128
TOK = 128
HG = 8
ROWS = HG * TOK
CHUNK = 256
NCHUNK = ROWS // CHUNK
NZ, NY = 8, 4
NH = 8
TOKDEV = 16
OWN = 16
LOG2E = 1.4426950408889634
LN2 = 0.6931471805599453
NEG = -1e30
SCALE = D**-0.5
F32 = jnp.float32
BF16 = jnp.bfloat16
MESH = pl.DeviceIdType.MESH


def dot(a, b):
    return jnp.dot(a, b, preferred_element_type=F32)


def kernel(
    q_hbm, k_hbm, v_hbm, g_hbm, doc_hbm, owner_hbm,
    att_ref, lse_ref, gq_ref, gk_ref, gv_ref,
    q_in, g_in, k_ref, v_ref, doc_ref, owner_ref,
    qt, gt, qs, gs, kv, stage, pbuf, dpb, dsb, ot, dqt, mrun, lrun, mgrp, delta,
    part, yrecv, total, pieces, hrecv, gathered, lown, lgat,
    load_sem, ha_send, ha_recv, kz_send, ky_send, kv_recv,
    gy_send, gy_recv, hb_send, hb_recv, ly_send, ly_recv, lz_send, lz_recv,
):
    ctx = lax.axis_index("ctx")
    head = lax.axis_index("head")
    z = ctx // NY
    y = ctx % NY

    loads = [
        pltpu.make_async_copy(src, dst, load_sem.at[i])
        for i, (src, dst) in enumerate(
            (
                (k_hbm, k_ref), (v_hbm, v_ref), (q_hbm, q_in), (g_hbm, g_in),
                (doc_hbm, doc_ref), (owner_hbm, owner_ref),
            )
        )
    ]
    for load in loads:
        load.start()

    def at_head(i):
        return (ctx, (head + i) % NH)

    def at_y(i):
        return (z * NY + (y + i) % NY, head)

    def at_z(i):
        return (((z + i) % NZ) * NY + y, head)

    barrier = pltpu.get_barrier_semaphore()
    for i in range(1, NH):
        pl.semaphore_signal(barrier, inc=1, device_id=at_head(i), device_id_type=MESH)
    for i in range(1, NY):
        pl.semaphore_signal(barrier, inc=1, device_id=at_y(i), device_id_type=MESH)
    for i in (1, 2, 4):

        @pl.when(z >= i)
        def _(i=i):
            pl.semaphore_signal(barrier, inc=1, device_id=at_z(NZ - i), device_id_type=MESH)


    for i in (5, 6, 7):

        @pl.when(z < NZ - i)
        def _(i=i):
            pl.semaphore_signal(barrier, inc=1, device_id=at_z(i), device_id_type=MESH)

    loads[0].wait()
    loads[1].wait()
    for h in range(NH):
        stage[h, 0] = k_ref[:, h * D : (h + 1) * D]
        stage[h, 1] = v_ref[:, h * D : (h + 1) * D]
    above = sum((z < NZ - i).astype(jnp.int32) for i in (1, 2, 4))
    below = sum((z >= i).astype(jnp.int32) for i in (5, 6, 7))
    pl.semaphore_wait(barrier, NH + NY - 2 + above + below)

    def remote(src, dst, ssem, rsem, to):
        return pltpu.make_async_remote_copy(
            src_ref=src, dst_ref=dst, send_sem=ssem, recv_sem=rsem, device_id=to, device_id_type=MESH
        )

    def head_copy(i):
        to = (head + i) % NH
        rows = pl.ds(pl.multiple_of(head * TOKDEV, TOKDEV), TOKDEV)
        return remote(
            stage.at[to], kv.at[OWN, :, rows, :], ha_send.at[i], ha_recv.at[i], at_head(i)
        )

    def head_arrival(i):
        rows = pl.ds(pl.multiple_of(((head + NH - i) % NH) * TOKDEV, TOKDEV), TOKDEV)
        return remote(stage.at[0], kv.at[OWN, :, rows, :], ha_send.at[i], ha_recv.at[i], at_head(i))

    for i in range(1, NH):
        head_copy(i).start()
    kv[OWN, :, pl.ds(pl.multiple_of(head * TOKDEV, TOKDEV), TOKDEV), :] = stage[head]

    for load in loads[2:]:
        load.wait()
    for h in range(HG):
        cols = slice(h * D, (h + 1) * D)
        qh, gh = q_in[:, cols], g_in[:, cols]
        qs[cols, :] = qh
        gs[cols, :] = gh
        qt[:, cols] = qh.T
        gt[:, cols] = gh.T

    @pl.when(z < 4)
    def _():
        for j in range(NY):

            @pl.when(y <= j)
            def _(j=j):
                kv[12 + j] = jnp.zeros((2, TOK, D), BF16)

    for i in range(1, NH):
        head_arrival(i).wait_recv()

    def level_copy(level, half):
        src = kv.at[4 + y, half] if level == 3 else kv.at[OWN, half]
        slot = 4 * (level - 1) + y
        step = 1 if level == 3 else level
        return remote(
            src, kv.at[slot, half], kz_send.at[half, level - 1], kv_recv.at[half, slot], at_z(step)
        )

    def level_goes(level):
        if level == 3:
            return (z >= 2) & (z < NZ - 1)
        return z < NZ - level

    def level_start(level, half):
        pl.when(level_goes(level))(lambda: level_copy(level, half).start())

    def spread_copy(level, half, i):
        src = kv.at[OWN, half] if level == 0 else kv.at[4 * (level - 1) + y, half]
        slot = 12 + y if level in (0, 4) else 4 * (level - 1) + y
        return remote(
            src, kv.at[slot, half], ky_send.at[half, 3 * level + i - 1], kv_recv.at[half, slot], at_y(i)
        )

    def spread_goes(level, i):
        if level == 0:
            return (y + i) < NY
        if level == 4:
            return (z >= 4) & ((y + i) >= NY)
        return z >= level

    def spread_start(level, half):
        for i in range(1, NY):
            pl.when(spread_goes(level, i))(lambda i=i: spread_copy(level, half, i).start())

    def slot_arrival(slot, half):
        ref = kv.at[slot, half]
        remote(ref, ref, kz_send.at[0, 0], kv_recv.at[half, slot], at_y(1)).wait_recv()

    for half in range(2):
        for level in (1, 2, 4):
            level_start(level, half)
        spread_start(0, half)

    docs = doc_ref[...]
    mine = doc_ref[pl.ds(ctx, 1), :]
    starts = jnp.zeros((1, TOK), F32)
    for v in range(1, 4):
        below = jnp.where(docs < v, 1.0, 0.0).astype(F32)
        count = jnp.sum(jnp.sum(below, axis=0, keepdims=True), axis=1, keepdims=True)
        starts = jnp.where(mine == v, count, starts)
    starts = jnp.concatenate([starts, starts], axis=1)
    tpos = lax.broadcasted_iota(jnp.int32, (1, TOK), 1).astype(F32)
    tpos = jnp.concatenate([tpos, tpos], axis=1) + (ctx * TOK).astype(F32)

    def positions(bases):
        step = lax.broadcasted_iota(jnp.int32, (TOK, 1), 0).astype(F32)
        return jnp.concatenate([step + b.astype(F32) for b in bases], axis=0)

    def chunk_of(c):
        return slice(c * CHUNK, (c + 1) * CHUNK)

    def score(group, slot0, count, bases, diagonal=False):
        n = count * TOK
        span = slice(slot0 * TOK, slot0 * TOK + n)
        keys = kv[slot0 : slot0 + count, 0].reshape(n, D)
        kpos = positions(bases)

        def step(c):
            cols = chunk_of(c)
            s = dot(keys, qt[:, cols]) * (SCALE * LOG2E)
            allowed = kpos >= starts
            if diagonal:
                allowed = allowed & (kpos <= tpos)
            s = jnp.where(allowed, s, NEG)
            top = jnp.max(s, axis=0, keepdims=True)
            if not diagonal:
                before = mrun[:, cols]
                top = jnp.maximum(before, top)
            p = jnp.exp2(s - top)
            mass = jnp.sum(p, axis=0, keepdims=True)
            if not diagonal:
                mass += lrun[:, cols] * jnp.exp2(before - top)
            pbuf[span, cols] = p.astype(BF16)
            lrun[:, cols] = mass
            mrun[:, cols] = top
            mgrp[group : group + 1, cols] = top

        for c in range(NCHUNK):
            step(c)

    def normalise(group, slot0, count):
        span = slice(slot0 * TOK, (slot0 + count) * TOK)

        def step(c):
            cols = chunk_of(c)
            share = jnp.exp2(mgrp[group : group + 1, cols] - mrun[:, cols]) / lrun[:, cols]
            pbuf[span, cols] = (pbuf[span, cols].astype(F32) * share).astype(BF16)

        for c in range(NCHUNK):
            step(c)
        part[slot0 : slot0 + count, 1] = dot(pbuf[span, :], gs[...]).astype(BF16).reshape(count, TOK, D)

    def with_values(slot0, count, first=False):
        n = count * TOK
        span = slice(slot0 * TOK, slot0 * TOK + n)
        values = kv[slot0 : slot0 + count, 1].reshape(n, D)
        across = values.T

        def step(c):
            cols = chunk_of(c)
            dpb[span, cols] = dot(values, gt[:, cols])
            part_o = dot(across, pbuf[span, cols])
            if first:
                ot[:, cols] = part_o
            else:
                ot[:, cols] += part_o

        for c in range(NCHUNK):
            step(c)

    def level_bases(level):
        return [((z - level) * NY + j) * TOK for j in range(NY)]

    mix_bases = [jnp.where(j < y, z * NY + j, (z - 4) * NY + j) * TOK for j in range(NY)]

    def pass_on(level, half):
        pl.when(z >= level)(lambda: slot_arrival(4 * (level - 1) + y, half))
        if level == 2:
            level_start(3, half)
        spread_start(level, half)

    def await_level(level, half):
        @pl.when(z >= level)
        def _():
            for i in range(1, NY):
                slot_arrival(4 * (level - 1) + (y + i) % NY, half)

    def await_mix(half):
        for i in range(1, NY):
            other = (y + i) % NY
            pl.when((other < y) | (z >= 4))(lambda other=other: slot_arrival(12 + other, half))

    def at_level(level, fn, *args):
        pl.when(z >= level)(lambda: fn(*args))

    score(0, OWN, 1, [ctx * TOK], True)
    pass_on(1, 0)
    pass_on(2, 0)
    pass_on(4, 0)
    pass_on(1, 1)
    await_level(1, 0)
    at_level(1, score, 1, 0, 4, level_bases(1))
    pass_on(3, 0)
    pass_on(2, 1)
    await_level(2, 0)
    at_level(2, score, 2, 4, 4, level_bases(2))
    pass_on(4, 1)
    await_mix(0)
    score(4, 12, 4, mix_bases)
    pass_on(3, 1)
    await_level(3, 0)
    at_level(3, score, 3, 8, 4, level_bases(3))

    def grad_y(g, half, i):
        other = (y + i) % NY
        return remote(
            part.at[4 * g + other, half], yrecv.at[g, y, half], gy_send.at[half, 3 * g + i - 1],
            gy_recv.at[half, 4 * g + y], at_y(i),
        )

    def grad_y_goes(g, i, part_of=None):
        if g < 3:
            return z >= g + 1
        own_level, far_level = (y + i) >= NY, ((y + i) < NY) & (z >= 4)
        return {None: own_level | far_level, 0: own_level, 4: far_level}[part_of]

    def grad_y_start(g, half, part_of=None):
        for i in range(1, NY):
            pl.when(grad_y_goes(g, i, part_of))(lambda i=i: grad_y(g, half, i).start())

    def grad_y_arrival(g, other):
        for half in range(2):
            ref = yrecv.at[g, other, half]
            remote(ref, ref, gy_send.at[0, 0], gy_recv.at[half, 4 * g + other], at_y(1)).wait_recv()

    normalise(4, 12, 4)
    grad_y_start(3, 1, 4)
    at_level(3, normalise, 3, 8, 4)
    grad_y_start(2, 1)
    at_level(2, normalise, 2, 4, 4)
    grad_y_start(1, 1)
    at_level(1, normalise, 1, 0, 4)
    grad_y_start(0, 1)
    grad_y_start(3, 1, 0)
    normalise(0, OWN, 1)

    norm = mrun[...] * LN2 + jnp.log(lrun[...])
    for h in range(HG):
        cols = slice(h * D, (h + 1) * D)
        lown[h : h + 1, :] = norm[:, cols]
    reps = lax.broadcasted_iota(jnp.int32, (32, TOK), 1) // 4 == lax.broadcasted_iota(
        jnp.int32, (32, TOK), 0
    )
    owners = dot(owner_ref[pl.ds(ctx, 1), :].astype(F32), jnp.where(reps, 1.0, 0.0).astype(F32))
    to_col = lax.broadcasted_iota(jnp.int32, (TOK, TOK), 0)
    from_tok = lax.broadcasted_iota(jnp.int32, (TOK, TOK), 1)
    hit = (owners == (to_col // 4).astype(F32)) & (to_col % 4 == from_tok % 4)
    lgat[z, y] = lax.dot_general(
        lown[...],
        jnp.where(hit, 1.0, 0.0).astype(F32),
        (((1,), (1,)), ((), ())),
        precision=lax.Precision.HIGHEST,
        preferred_element_type=F32,
    )

    def lse_y(i):
        return remote(lgat.at[z, y], lgat.at[z, y], ly_send.at[i], ly_recv.at[i], at_y(i))

    def lse_y_arrival(i):
        other = (y + NY - i) % NY
        return remote(lgat.at[z, other], lgat.at[z, other], ly_send.at[i], ly_recv.at[i], at_y(i))

    def lse_z(i):
        return remote(lgat.at[z], lgat.at[z], lz_send.at[i], lz_recv.at[i], at_z(i))

    def lse_z_arrival(i):
        block = lgat.at[(z + NZ - i) % NZ]
        return remote(block, block, lz_send.at[i], lz_recv.at[i], at_z(i))

    def lse_down():
        for i in range(1, NY):
            lse_y_arrival(i).wait_recv()
        for i in range(1, NZ):
            pl.when(z >= NZ - i)(lambda i=i: lse_z(i).start())
        for i in (1, 2, 4):
            pl.when(z < NZ - i)(lambda i=i: lse_z(i).start())

    relays = {3: (2, 1), 5: (4, 1), 6: (4, 2), 7: (6, 1)}

    def lse_relay(far):
        back, step = relays[far]
        block = lgat.at[(z + NZ - back) % NZ]
        return remote(block, block, lz_send.at[NZ + far], lz_recv.at[far], at_z(step))

    def lse_relay_goes(far):
        back, step = relays[far]
        return (z >= back) & (z < NZ - step)

    def lse_pass(*fars):
        for i in sorted({relays[far][0] for far in fars}):
            pl.when(z >= i)(lambda i=i: lse_z_arrival(i).wait_recv())
        for far in fars:
            pl.when(lse_relay_goes(far))(lambda far=far: lse_relay(far).start())

    for i in range(1, NY):
        lse_y(i).start()

    with_values(OWN, 1, True)
    await_level(1, 1)
    at_level(1, with_values, 0, 4)
    await_level(2, 1)
    at_level(2, with_values, 4, 4)
    await_mix(1)
    with_values(12, 4)
    await_level(3, 1)
    at_level(3, with_values, 8, 4)

    def finish(c):
        cols = chunk_of(c)
        full = ot[:, cols].astype(BF16).astype(F32)
        ot[:, cols] = full
        delta[:, cols] = jnp.sum(gt[:, cols].astype(F32) * full, axis=0, keepdims=True)

    for c in range(NCHUNK):
        finish(c)

    def backward(slot0, count):
        span = slice(slot0 * TOK, (slot0 + count) * TOK)

        def step(c):
            cols = chunk_of(c)
            slope = dpb[span, cols] - delta[:, cols]
            dsb[span, cols] = (pbuf[span, cols].astype(F32) * slope).astype(BF16)

        for c in range(NCHUNK):
            step(c)
        part[slot0 : slot0 + count, 0] = dot(dsb[span, :], qs[...]).astype(BF16).reshape(count, TOK, D)

    def query_gradient(slot0, count, first):
        span = slice(slot0 * TOK, (slot0 + count) * TOK)
        across = kv[slot0 : slot0 + count, 0].reshape(count * TOK, D).T

        def step(c):
            cols = chunk_of(c)
            dq = dot(across, dsb[span, cols])
            if first:
                dqt[:, cols] = dq
            else:
                dqt[:, cols] += dq

        for c in range(NCHUNK):
            step(c)

    def wide(ref, *at):
        return ref[at].astype(F32)

    def column_sum(level):
        g = level - 1
        total[...] = wide(part, 4 * g + y)
        for i in range(1, NY):
            other = (y + i) % NY
            if level == 4:

                @pl.when(other < y)
                def _(other=other):
                    grad_y_arrival(g, other)
                    total[...] += wide(yrecv, g, other)
            else:
                grad_y_arrival(g, other)
                total[...] += wide(yrecv, g, other)

    def home_rows(to):
        return pl.ds(pl.multiple_of(to * TOKDEV, TOKDEV), TOKDEV)

    def home(level, i):
        to = (head + i) % NH
        return remote(
            pieces.at[level, :, home_rows(to), :], hrecv.at[level, head],
            hb_send.at[level, i], hb_recv.at[level, i], (jnp.maximum(z - level, 0) * NY + y, to),
        )

    def home_arrival(level, i):
        ref = hrecv.at[level, (head + NH - i) % NH]
        return remote(ref, ref, hb_send.at[level, i], hb_recv.at[level, i], at_head(1))

    def home_start(level):
        pieces[level, 0] = (total[0] * SCALE).astype(BF16)
        pieces[level, 1] = total[1].astype(BF16)
        for i in range(0 if level else 1, NH):
            home(level, i).start()

    def reduce_level(level):
        @pl.when(z >= level)
        def _():
            column_sum(level)
            home_start(level)

    backward(12, 4)
    grad_y_start(3, 0, 4)
    at_level(3, backward, 8, 4)
    grad_y_start(2, 0)
    at_level(2, backward, 4, 4)
    grad_y_start(1, 0)
    at_level(1, backward, 0, 4)
    grad_y_start(0, 0)
    grad_y_start(3, 0, 0)
    lse_down()
    reduce_level(4)
    backward(OWN, 1)
    query_gradient(OWN, 1, True)
    query_gradient(12, 4, False)
    reduce_level(3)
    lse_pass(3, 5, 6)
    at_level(3, query_gradient, 8, 4, False)
    for h in range(HG):
        cols = slice(h * D, (h + 1) * D)
        att_ref[:, cols] = ot[:, cols].T.astype(BF16)
    at_level(2, query_gradient, 4, 4, False)
    at_level(1, query_gradient, 0, 4, False)
    reduce_level(2)
    lse_pass(7)
    for h in range(HG):
        cols = slice(h * D, (h + 1) * D)
        gq_ref[:, cols] = (dqt[:, cols] * SCALE).T.astype(BF16)

    reduce_level(1)
    total[...] = wide(part, OWN)
    for i in range(1, NY):
        other = (y + i) % NY

        @pl.when(other > y)
        def _(other=other):
            grad_y_arrival(3, other)
            total[...] += wide(yrecv, 3, other)

    home_start(0)
    hrecv[0, head] = pieces[0, :, home_rows(head), :]

    for i in range(1, NZ):
        if i in (2, 4, 6):
            pl.when(z < i)(lambda i=i: lse_z_arrival(i).wait_recv())
        else:
            lse_z_arrival(i).wait_recv()
    lane = lax.broadcasted_iota(jnp.int32, (HG, TOK), 1) // 4
    owned = jnp.zeros((HG, TOK), F32)
    for d in range(NZ * NY):
        moved = pltpu.roll(lgat[d // NY, d % NY], ((d - ctx) * 4) % TOK, 1)
        owned = jnp.where(lane == d, moved, owned)
    lse_ref[...] = owned

    for i in range(1, NH):
        head_copy(i).wait_send()
    for hop in range(1, 5):

        @pl.when(level_goes(hop))
        def _(hop=hop):
            for half in range(2):
                level_copy(hop, half).wait_send()

    for level in range(5):
        for i in range(1, NY):

            @pl.when(spread_goes(level, i))
            def _(level=level, i=i):
                for half in range(2):
                    spread_copy(level, half, i).wait_send()

    for g in range(4):
        for i in range(1, NY):

            @pl.when(grad_y_goes(g, i))
            def _(g=g, i=i):
                for half in range(2):
                    grad_y(g, half, i).wait_send()

    for i in range(1, NY):
        lse_y(i).wait_send()
    for i in range(1, NZ):
        if i in relays:
            pl.when(z >= NZ - i)(lambda i=i: lse_z(i).wait_send())
            pl.when(lse_relay_goes(i))(lambda i=i: lse_relay(i).wait_send())
        else:
            lse_z(i).wait_send()

    for i in range(1, NH):
        home_arrival(0, i).wait_recv()
    gathered[...] = wide(hrecv, 0)
    for level in range(1, 5):

        @pl.when(z < NZ - level)
        def _(level=level):
            for i in range(NH):
                home_arrival(level, i).wait_recv()
            gathered[...] += wide(hrecv, level)

    for h in range(NH):
        cols = slice(h * D, (h + 1) * D)
        gk_ref[:, cols] = gathered[h, 0].astype(BF16)
        gv_ref[:, cols] = gathered[h, 1].astype(BF16)

    for level in range(1, 5):

        @pl.when(z >= level)
        def _(level=level):
            for i in range(NH):
                home(level, i).wait_send()

    for i in range(1, NH):
        home(0, i).wait_send()


def deliver(*refs):
    sem = refs[-1]
    copies = [pltpu.make_async_copy(refs[i], refs[5 + i], sem.at[i]) for i in range(5)]
    for copy in copies:
        copy.start()
    for copy in copies:
        copy.wait()


def body(queries, key_rows, value_rows, grad_out, doc_ids, block_owner):
    hbm = pl.BlockSpec(memory_space=pltpu.HBM)
    dma = pltpu.SemaphoreType.DMA
    keys = 17 * TOK
    shapes = (
        jax.ShapeDtypeStruct((TOK, ROWS), BF16),
        jax.ShapeDtypeStruct((HG, TOK), F32),
        jax.ShapeDtypeStruct((TOK, ROWS), BF16),
        jax.ShapeDtypeStruct((TOKDEV, NH * D), BF16),
        jax.ShapeDtypeStruct((TOKDEV, NH * D), BF16),
    )
    arrays = (queries, key_rows, value_rows, grad_out, doc_ids.reshape(32, TOK), block_owner)
    outs = pl.pallas_call(
        kernel,
        out_shape=shapes,
        in_specs=[hbm] * 6,
        out_specs=(pl.BlockSpec(memory_space=pltpu.VMEM),) * 5,
        scratch_shapes=[
            pltpu.VMEM((TOK, ROWS), BF16),
            pltpu.VMEM((TOK, ROWS), BF16),
            pltpu.VMEM((TOKDEV, NH * D), BF16),
            pltpu.VMEM((TOKDEV, NH * D), BF16),
            pltpu.VMEM((32, TOK), jnp.int32),
            pltpu.VMEM((32, 32), jnp.int32),
            pltpu.VMEM((D, ROWS), BF16),
            pltpu.VMEM((D, ROWS), BF16),
            pltpu.VMEM((ROWS, D), BF16),
            pltpu.VMEM((ROWS, D), BF16),
            pltpu.VMEM((17, 2, TOK, D), BF16),
            pltpu.VMEM((NH, 2, TOKDEV, D), BF16),
            pltpu.VMEM((keys, ROWS), BF16),
            pltpu.VMEM((keys, ROWS), F32),
            pltpu.VMEM((keys, ROWS), BF16),
            pltpu.VMEM((D, ROWS), F32),
            pltpu.VMEM((D, ROWS), F32),
            pltpu.VMEM((1, ROWS), F32),
            pltpu.VMEM((1, ROWS), F32),
            pltpu.VMEM((8, ROWS), F32),
            pltpu.VMEM((1, ROWS), F32),
            pltpu.VMEM((17, 2, TOK, D), BF16),
            pltpu.VMEM((4, NY, 2, TOK, D), BF16),
            pltpu.VMEM((2, TOK, D), F32),
            pltpu.VMEM((5, 2, TOK, D), BF16),
            pltpu.VMEM((5, NH, 2, TOKDEV, D), BF16),
            pltpu.VMEM((NH, 2, TOKDEV, D), F32),
            pltpu.VMEM((HG, TOK), F32),
            pltpu.VMEM((NZ, NY, HG, TOK), F32),
            dma((6,)),
            dma((NH,)), dma((NH,)),
            dma((2, 4)), dma((2, 15)), dma((2, 17)),
            dma((2, 12)), dma((2, 16)),
            dma((5, NH)), dma((5, NH)),
            dma((NY,)), dma((NY,)), dma((2 * NZ,)), dma((NZ,)),
        ],
        compiler_params=pltpu.CompilerParams(
            collective_id=0, has_side_effects=True, vmem_limit_bytes=48 * 1024 * 1024
        ),
        name="packed_attention",
    )(*(pltpu.with_memory_space_constraint(a, pltpu.HBM) for a in arrays))
    return pl.pallas_call(
        deliver,
        out_shape=shapes,
        in_specs=[pl.BlockSpec(memory_space=pltpu.VMEM)] * 5,
        out_specs=(hbm,) * 5,
        scratch_shapes=[dma((5,))],
        compiler_params=pltpu.CompilerParams(vmem_limit_bytes=2 * 1024 * 1024),
        name="deliver",
    )(*outs)


def solution(mesh):
    return jax.shard_map(
        body,
        mesh=mesh,
        in_specs=(
            P("ctx", "head"), P(("ctx", "head"), None), P(("ctx", "head"), None),
            P("ctx", "head"), P(), P(),
        ),
        out_specs=(
            P("ctx", "head"), P("head", "ctx"), P("ctx", "head"),
            P(("ctx", "head"), None), P(("ctx", "head"), None),
        ),
        check_vma=False,
    )
```

```python
import jax
import jax.numpy as jnp
from jax import lax
from jax.experimental import pallas as pl
from jax.experimental.pallas import tpu as pltpu
from jax.sharding import PartitionSpec as P

D = 128
TOK = 128
HG = 8
ROWS = HG * TOK
CHUNK = 256
NCHUNK = ROWS // CHUNK
NZ, NY = 8, 4
NH = 8
TOKDEV = 16
OWN = 16
LOG2E = 1.4426950408889634
LN2 = 0.6931471805599453
NEG = -1e30
SCALE = D**-0.5
F32 = jnp.float32
BF16 = jnp.bfloat16
MESH = pl.DeviceIdType.MESH


def dot(a, b):
    return jnp.dot(a, b, preferred_element_type=F32)


def kernel(
    q_hbm, k_hbm, v_hbm, g_hbm, doc_hbm, owner_hbm,
    att_ref, lse_ref, gq_ref, gk_ref, gv_ref,
    q_in, g_in, k_ref, v_ref, doc_ref, owner_ref,
    qt, gt, qs, gs, kv, stage, pbuf, dpb, dsb, ot, dqt, mrun, lrun, mgrp, delta,
    part, yrecv, total, pieces, hrecv, gathered, lown, lgat,
    load_sem, ha_send, ha_recv, kz_send, ky_send, kv_recv,
    gy_send, gy_recv, hb_send, hb_recv, ly_send, ly_recv, lz_send, lz_recv,
):
    ctx = lax.axis_index("ctx")
    head = lax.axis_index("head")
    z = ctx // NY
    y = ctx % NY

    loads = [
        pltpu.make_async_copy(src, dst, load_sem.at[i])
        for i, (src, dst) in enumerate(
            (
                (k_hbm, k_ref), (v_hbm, v_ref), (q_hbm, q_in), (g_hbm, g_in),
                (doc_hbm, doc_ref), (owner_hbm, owner_ref),
            )
        )
    ]
    for load in loads:
        load.start()

    def at_head(i):
        return (ctx, (head + i) % NH)

    def at_y(i):
        return (z * NY + (y + i) % NY, head)

    def at_z(i):
        return (((z + i) % NZ) * NY + y, head)

    barrier = pltpu.get_barrier_semaphore()
    for i in range(1, NH):
        pl.semaphore_signal(barrier, inc=1, device_id=at_head(i), device_id_type=MESH)
    for i in range(1, NY):
        pl.semaphore_signal(barrier, inc=1, device_id=at_y(i), device_id_type=MESH)
    for i in (1, 2, 4):

        @pl.when(z >= i)
        def _(i=i):
            pl.semaphore_signal(barrier, inc=1, device_id=at_z(NZ - i), device_id_type=MESH)


    for i in (5, 6, 7):

        @pl.when(z < NZ - i)
        def _(i=i):
            pl.semaphore_signal(barrier, inc=1, device_id=at_z(i), device_id_type=MESH)

    loads[0].wait()
    loads[1].wait()
    for h in range(NH):
        stage[h, 0] = k_ref[:, h * D : (h + 1) * D]
        stage[h, 1] = v_ref[:, h * D : (h + 1) * D]
    above = sum((z < NZ - i).astype(jnp.int32) for i in (1, 2, 4))
    below = sum((z >= i).astype(jnp.int32) for i in (5, 6, 7))
    pl.semaphore_wait(barrier, NH + NY - 2 + above + below)

    def remote(src, dst, ssem, rsem, to):
        return pltpu.make_async_remote_copy(
            src_ref=src, dst_ref=dst, send_sem=ssem, recv_sem=rsem, device_id=to, device_id_type=MESH
        )

    def head_copy(i):
        to = (head + i) % NH
        rows = pl.ds(pl.multiple_of(head * TOKDEV, TOKDEV), TOKDEV)
        return remote(
            stage.at[to], kv.at[OWN, :, rows, :], ha_send.at[i], ha_recv.at[i], at_head(i)
        )

    def head_arrival(i):
        rows = pl.ds(pl.multiple_of(((head + NH - i) % NH) * TOKDEV, TOKDEV), TOKDEV)
        return remote(stage.at[0], kv.at[OWN, :, rows, :], ha_send.at[i], ha_recv.at[i], at_head(i))

    for i in range(1, NH):
        head_copy(i).start()
    kv[OWN, :, pl.ds(pl.multiple_of(head * TOKDEV, TOKDEV), TOKDEV), :] = stage[head]

    for load in loads[2:]:
        load.wait()
    for h in range(HG):
        cols = slice(h * D, (h + 1) * D)
        qh, gh = q_in[:, cols], g_in[:, cols]
        qs[cols, :] = qh
        gs[cols, :] = gh
        qt[:, cols] = qh.T
        gt[:, cols] = gh.T

    @pl.when(z < 4)
    def _():
        for j in range(NY):

            @pl.when(y <= j)
            def _(j=j):
                kv[12 + j] = jnp.zeros((2, TOK, D), BF16)

    for i in range(1, NH):
        head_arrival(i).wait_recv()

    def level_copy(level, half):
        src = kv.at[4 + y, half] if level == 3 else kv.at[OWN, half]
        slot = 4 * (level - 1) + y
        step = 1 if level == 3 else level
        return remote(
            src, kv.at[slot, half], kz_send.at[half, level - 1], kv_recv.at[half, slot], at_z(step)
        )

    def level_goes(level):
        if level == 3:
            return (z >= 2) & (z < NZ - 1)
        return z < NZ - level

    def level_start(level, half):
        pl.when(level_goes(level))(lambda: level_copy(level, half).start())

    def spread_copy(level, half, i):
        src = kv.at[OWN, half] if level == 0 else kv.at[4 * (level - 1) + y, half]
        slot = 12 + y if level in (0, 4) else 4 * (level - 1) + y
        return remote(
            src, kv.at[slot, half], ky_send.at[half, 3 * level + i - 1], kv_recv.at[half, slot], at_y(i)
        )

    def spread_goes(level, i):
        if level == 0:
            return (y + i) < NY
        if level == 4:
            return (z >= 4) & ((y + i) >= NY)
        return z >= level

    def spread_start(level, half):
        for i in range(1, NY):
            pl.when(spread_goes(level, i))(lambda i=i: spread_copy(level, half, i).start())

    def slot_arrival(slot, half):
        ref = kv.at[slot, half]
        remote(ref, ref, kz_send.at[0, 0], kv_recv.at[half, slot], at_y(1)).wait_recv()

    for half in range(2):
        for level in (1, 2, 4):
            level_start(level, half)
        spread_start(0, half)

    docs = doc_ref[...]
    mine = doc_ref[pl.ds(ctx, 1), :]
    starts = jnp.zeros((1, TOK), F32)
    for v in range(1, 4):
        below = jnp.where(docs < v, 1.0, 0.0).astype(F32)
        count = jnp.sum(jnp.sum(below, axis=0, keepdims=True), axis=1, keepdims=True)
        starts = jnp.where(mine == v, count, starts)
    starts = jnp.concatenate([starts, starts], axis=1)
    tpos = lax.broadcasted_iota(jnp.int32, (1, TOK), 1).astype(F32)
    tpos = jnp.concatenate([tpos, tpos], axis=1) + (ctx * TOK).astype(F32)

    def positions(bases):
        step = lax.broadcasted_iota(jnp.int32, (TOK, 1), 0).astype(F32)
        return jnp.concatenate([step + b.astype(F32) for b in bases], axis=0)

    def chunk_of(c):
        return slice(c * CHUNK, (c + 1) * CHUNK)

    def score(group, slot0, count, bases, diagonal=False):
        n = count * TOK
        span = slice(slot0 * TOK, slot0 * TOK + n)
        keys = kv[slot0 : slot0 + count, 0].reshape(n, D)
        kpos = positions(bases)

        def step(c):
            cols = chunk_of(c)
            s = dot(keys, qt[:, cols]) * (SCALE * LOG2E)
            allowed = kpos >= starts
            if diagonal:
                allowed = allowed & (kpos <= tpos)
            s = jnp.where(allowed, s, NEG)
            top = jnp.max(s, axis=0, keepdims=True)
            if not diagonal:
                before = mrun[:, cols]
                top = jnp.maximum(before, top)
            p = jnp.exp2(s - top)
            mass = jnp.sum(p, axis=0, keepdims=True)
            if not diagonal:
                mass += lrun[:, cols] * jnp.exp2(before - top)
            pbuf[span, cols] = p.astype(BF16)
            lrun[:, cols] = mass
            mrun[:, cols] = top
            mgrp[group : group + 1, cols] = top

        for c in range(NCHUNK):
            step(c)

    def normalise(group, slot0, count):
        span = slice(slot0 * TOK, (slot0 + count) * TOK)

        def step(c):
            cols = chunk_of(c)
            share = jnp.exp2(mgrp[group : group + 1, cols] - mrun[:, cols]) / lrun[:, cols]
            pbuf[span, cols] = (pbuf[span, cols].astype(F32) * share).astype(BF16)

        for c in range(NCHUNK):
            step(c)
        part[slot0 : slot0 + count, 1] = dot(pbuf[span, :], gs[...]).astype(BF16).reshape(count, TOK, D)

    def with_values(slot0, count, first=False):
        n = count * TOK
        span = slice(slot0 * TOK, slot0 * TOK + n)
        values = kv[slot0 : slot0 + count, 1].reshape(n, D)
        across = values.T

        def step(c):
            cols = chunk_of(c)
            dpb[span, cols] = dot(values, gt[:, cols])
            part_o = dot(across, pbuf[span, cols])
            if first:
                ot[:, cols] = part_o
            else:
                ot[:, cols] += part_o

        for c in range(NCHUNK):
            step(c)

    def level_bases(level):
        return [((z - level) * NY + j) * TOK for j in range(NY)]

    mix_bases = [jnp.where(j < y, z * NY + j, (z - 4) * NY + j) * TOK for j in range(NY)]

    def pass_on(level, half):
        pl.when(z >= level)(lambda: slot_arrival(4 * (level - 1) + y, half))
        if level == 2:
            level_start(3, half)
        spread_start(level, half)

    def await_level(level, half):
        @pl.when(z >= level)
        def _():
            for i in range(1, NY):
                slot_arrival(4 * (level - 1) + (y + i) % NY, half)

    def await_mix(half):
        for i in range(1, NY):
            other = (y + i) % NY
            pl.when((other < y) | (z >= 4))(lambda other=other: slot_arrival(12 + other, half))

    def at_level(level, fn, *args):
        pl.when(z >= level)(lambda: fn(*args))

    score(0, OWN, 1, [ctx * TOK], True)
    pass_on(1, 0)
    pass_on(2, 0)
    pass_on(4, 0)
    await_level(1, 0)
    at_level(1, score, 1, 0, 4, level_bases(1))
    pass_on(3, 0)
    pass_on(1, 1)
    pass_on(2, 1)
    await_level(2, 0)
    at_level(2, score, 2, 4, 4, level_bases(2))
    pass_on(4, 1)
    await_mix(0)
    score(4, 12, 4, mix_bases)
    pass_on(3, 1)
    await_level(3, 0)
    at_level(3, score, 3, 8, 4, level_bases(3))

    def grad_y(g, half, i):
        other = (y + i) % NY
        return remote(
            part.at[4 * g + other, half], yrecv.at[g, y, half], gy_send.at[half, 3 * g + i - 1],
            gy_recv.at[half, 4 * g + y], at_y(i),
        )

    def grad_y_goes(g, i, part_of=None):
        if g < 3:
            return z >= g + 1
        own_level, far_level = (y + i) >= NY, ((y + i) < NY) & (z >= 4)
        return {None: own_level | far_level, 0: own_level, 4: far_level}[part_of]

    def grad_y_start(g, half, part_of=None):
        for i in range(1, NY):
            pl.when(grad_y_goes(g, i, part_of))(lambda i=i: grad_y(g, half, i).start())

    def grad_y_arrival(g, other):
        for half in range(2):
            ref = yrecv.at[g, other, half]
            remote(ref, ref, gy_send.at[0, 0], gy_recv.at[half, 4 * g + other], at_y(1)).wait_recv()

    normalise(4, 12, 4)
    grad_y_start(3, 1, 4)
    at_level(3, normalise, 3, 8, 4)
    grad_y_start(2, 1)
    at_level(2, normalise, 2, 4, 4)
    grad_y_start(1, 1)
    at_level(1, normalise, 1, 0, 4)
    grad_y_start(0, 1)
    grad_y_start(3, 1, 0)
    normalise(0, OWN, 1)

    norm = mrun[...] * LN2 + jnp.log(lrun[...])
    for h in range(HG):
        cols = slice(h * D, (h + 1) * D)
        lown[h : h + 1, :] = norm[:, cols]
    reps = lax.broadcasted_iota(jnp.int32, (32, TOK), 1) // 4 == lax.broadcasted_iota(
        jnp.int32, (32, TOK), 0
    )
    owners = dot(owner_ref[pl.ds(ctx, 1), :].astype(F32), jnp.where(reps, 1.0, 0.0).astype(F32))
    to_col = lax.broadcasted_iota(jnp.int32, (TOK, TOK), 0)
    from_tok = lax.broadcasted_iota(jnp.int32, (TOK, TOK), 1)
    hit = (owners == (to_col // 4).astype(F32)) & (to_col % 4 == from_tok % 4)
    lgat[z, y] = lax.dot_general(
        lown[...],
        jnp.where(hit, 1.0, 0.0).astype(F32),
        (((1,), (1,)), ((), ())),
        precision=lax.Precision.HIGHEST,
        preferred_element_type=F32,
    )

    def lse_y(i):
        return remote(lgat.at[z, y], lgat.at[z, y], ly_send.at[i], ly_recv.at[i], at_y(i))

    def lse_y_arrival(i):
        other = (y + NY - i) % NY
        return remote(lgat.at[z, other], lgat.at[z, other], ly_send.at[i], ly_recv.at[i], at_y(i))

    def lse_z(i):
        return remote(lgat.at[z], lgat.at[z], lz_send.at[i], lz_recv.at[i], at_z(i))

    def lse_z_arrival(i):
        block = lgat.at[(z + NZ - i) % NZ]
        return remote(block, block, lz_send.at[i], lz_recv.at[i], at_z(i))

    def lse_down():
        for i in range(1, NY):
            lse_y_arrival(i).wait_recv()
        for i in range(1, NZ):
            pl.when(z >= NZ - i)(lambda i=i: lse_z(i).start())

    def lse_up():
        for i in range(1, NZ):

            @pl.when(z < NZ - i)
            def _(i=i):
                lse_z_arrival(NZ - i).wait_recv()
                lse_z(i).start()

    for i in range(1, NY):
        lse_y(i).start()

    with_values(OWN, 1, True)
    await_level(1, 1)
    at_level(1, with_values, 0, 4)
    await_level(2, 1)
    at_level(2, with_values, 4, 4)
    await_mix(1)
    with_values(12, 4)
    await_level(3, 1)
    at_level(3, with_values, 8, 4)

    def finish(c):
        cols = chunk_of(c)
        full = ot[:, cols].astype(BF16).astype(F32)
        ot[:, cols] = full
        delta[:, cols] = jnp.sum(gt[:, cols].astype(F32) * full, axis=0, keepdims=True)

    for c in range(NCHUNK):
        finish(c)

    def backward(slot0, count):
        span = slice(slot0 * TOK, (slot0 + count) * TOK)

        def step(c):
            cols = chunk_of(c)
            slope = dpb[span, cols] - delta[:, cols]
            dsb[span, cols] = (pbuf[span, cols].astype(F32) * slope).astype(BF16)

        for c in range(NCHUNK):
            step(c)
        part[slot0 : slot0 + count, 0] = dot(dsb[span, :], qs[...]).astype(BF16).reshape(count, TOK, D)

    def query_gradient(slot0, count, first):
        span = slice(slot0 * TOK, (slot0 + count) * TOK)
        across = kv[slot0 : slot0 + count, 0].reshape(count * TOK, D).T

        def step(c):
            cols = chunk_of(c)
            dq = dot(across, dsb[span, cols])
            if first:
                dqt[:, cols] = dq
            else:
                dqt[:, cols] += dq

        for c in range(NCHUNK):
            step(c)

    def wide(ref, *at):
        return ref[at].astype(F32)

    def column_sum(level):
        g = level - 1
        total[...] = wide(part, 4 * g + y)
        for i in range(1, NY):
            other = (y + i) % NY
            if level == 4:

                @pl.when(other < y)
                def _(other=other):
                    grad_y_arrival(g, other)
                    total[...] += wide(yrecv, g, other)
            else:
                grad_y_arrival(g, other)
                total[...] += wide(yrecv, g, other)

    def home_rows(to):
        return pl.ds(pl.multiple_of(to * TOKDEV, TOKDEV), TOKDEV)

    def home(level, i):
        to = (head + i) % NH
        return remote(
            pieces.at[level, :, home_rows(to), :], hrecv.at[level, head],
            hb_send.at[level, i], hb_recv.at[level, i], (jnp.maximum(z - level, 0) * NY + y, to),
        )

    def home_arrival(level, i):
        ref = hrecv.at[level, (head + NH - i) % NH]
        return remote(ref, ref, hb_send.at[level, i], hb_recv.at[level, i], at_head(1))

    def home_start(level):
        pieces[level, 0] = (total[0] * SCALE).astype(BF16)
        pieces[level, 1] = total[1].astype(BF16)
        for i in range(0 if level else 1, NH):
            home(level, i).start()

    def reduce_level(level):
        @pl.when(z >= level)
        def _():
            column_sum(level)
            home_start(level)

    backward(12, 4)
    grad_y_start(3, 0, 4)
    at_level(3, backward, 8, 4)
    grad_y_start(2, 0)
    at_level(2, backward, 4, 4)
    grad_y_start(1, 0)
    at_level(1, backward, 0, 4)
    grad_y_start(0, 0)
    grad_y_start(3, 0, 0)
    lse_down()
    reduce_level(4)
    backward(OWN, 1)
    query_gradient(OWN, 1, True)
    query_gradient(12, 4, False)
    reduce_level(3)
    at_level(3, query_gradient, 8, 4, False)
    for h in range(HG):
        cols = slice(h * D, (h + 1) * D)
        att_ref[:, cols] = ot[:, cols].T.astype(BF16)
    at_level(2, query_gradient, 4, 4, False)
    at_level(1, query_gradient, 0, 4, False)
    reduce_level(2)
    for h in range(HG):
        cols = slice(h * D, (h + 1) * D)
        gq_ref[:, cols] = (dqt[:, cols] * SCALE).T.astype(BF16)

    reduce_level(1)
    lse_up()
    total[...] = wide(part, OWN)
    for i in range(1, NY):
        other = (y + i) % NY

        @pl.when(other > y)
        def _(other=other):
            grad_y_arrival(3, other)
            total[...] += wide(yrecv, 3, other)

    home_start(0)
    hrecv[0, head] = pieces[0, :, home_rows(head), :]

    for i in range(1, NZ):
        pl.when(z >= i)(lambda i=i: lse_z_arrival(i).wait_recv())
    lane = lax.broadcasted_iota(jnp.int32, (HG, TOK), 1) // 4
    owned = jnp.zeros((HG, TOK), F32)
    for d in range(NZ * NY):
        moved = pltpu.roll(lgat[d // NY, d % NY], ((d - ctx) * 4) % TOK, 1)
        owned = jnp.where(lane == d, moved, owned)
    lse_ref[...] = owned

    for i in range(1, NH):
        head_copy(i).wait_send()
    for hop in range(1, 5):

        @pl.when(level_goes(hop))
        def _(hop=hop):
            for half in range(2):
                level_copy(hop, half).wait_send()

    for level in range(5):
        for i in range(1, NY):

            @pl.when(spread_goes(level, i))
            def _(level=level, i=i):
                for half in range(2):
                    spread_copy(level, half, i).wait_send()

    for g in range(4):
        for i in range(1, NY):

            @pl.when(grad_y_goes(g, i))
            def _(g=g, i=i):
                for half in range(2):
                    grad_y(g, half, i).wait_send()

    for i in range(1, NY):
        lse_y(i).wait_send()
    for i in range(1, NZ):
        lse_z(i).wait_send()

    for i in range(1, NH):
        home_arrival(0, i).wait_recv()
    gathered[...] = wide(hrecv, 0)
    for level in range(1, 5):

        @pl.when(z < NZ - level)
        def _(level=level):
            for i in range(NH):
                home_arrival(level, i).wait_recv()
            gathered[...] += wide(hrecv, level)

    for h in range(NH):
        cols = slice(h * D, (h + 1) * D)
        gk_ref[:, cols] = gathered[h, 0].astype(BF16)
        gv_ref[:, cols] = gathered[h, 1].astype(BF16)

    for level in range(1, 5):

        @pl.when(z >= level)
        def _(level=level):
            for i in range(NH):
                home(level, i).wait_send()

    for i in range(1, NH):
        home(0, i).wait_send()


def deliver(*refs):
    sem = refs[-1]
    copies = [pltpu.make_async_copy(refs[i], refs[5 + i], sem.at[i]) for i in range(5)]
    for copy in copies:
        copy.start()
    for copy in copies:
        copy.wait()


def body(queries, key_rows, value_rows, grad_out, doc_ids, block_owner):
    hbm = pl.BlockSpec(memory_space=pltpu.HBM)
    dma = pltpu.SemaphoreType.DMA
    keys = 17 * TOK
    shapes = (
        jax.ShapeDtypeStruct((TOK, ROWS), BF16),
        jax.ShapeDtypeStruct((HG, TOK), F32),
        jax.ShapeDtypeStruct((TOK, ROWS), BF16),
        jax.ShapeDtypeStruct((TOKDEV, NH * D), BF16),
        jax.ShapeDtypeStruct((TOKDEV, NH * D), BF16),
    )
    arrays = (queries, key_rows, value_rows, grad_out, doc_ids.reshape(32, TOK), block_owner)
    outs = pl.pallas_call(
        kernel,
        out_shape=shapes,
        in_specs=[hbm] * 6,
        out_specs=(pl.BlockSpec(memory_space=pltpu.VMEM),) * 5,
        scratch_shapes=[
            pltpu.VMEM((TOK, ROWS), BF16),
            pltpu.VMEM((TOK, ROWS), BF16),
            pltpu.VMEM((TOKDEV, NH * D), BF16),
            pltpu.VMEM((TOKDEV, NH * D), BF16),
            pltpu.VMEM((32, TOK), jnp.int32),
            pltpu.VMEM((32, 32), jnp.int32),
            pltpu.VMEM((D, ROWS), BF16),
            pltpu.VMEM((D, ROWS), BF16),
            pltpu.VMEM((ROWS, D), BF16),
            pltpu.VMEM((ROWS, D), BF16),
            pltpu.VMEM((17, 2, TOK, D), BF16),
            pltpu.VMEM((NH, 2, TOKDEV, D), BF16),
            pltpu.VMEM((keys, ROWS), BF16),
            pltpu.VMEM((keys, ROWS), F32),
            pltpu.VMEM((keys, ROWS), BF16),
            pltpu.VMEM((D, ROWS), F32),
            pltpu.VMEM((D, ROWS), F32),
            pltpu.VMEM((1, ROWS), F32),
            pltpu.VMEM((1, ROWS), F32),
            pltpu.VMEM((8, ROWS), F32),
            pltpu.VMEM((1, ROWS), F32),
            pltpu.VMEM((17, 2, TOK, D), BF16),
            pltpu.VMEM((4, NY, 2, TOK, D), BF16),
            pltpu.VMEM((2, TOK, D), F32),
            pltpu.VMEM((5, 2, TOK, D), BF16),
            pltpu.VMEM((5, NH, 2, TOKDEV, D), BF16),
            pltpu.VMEM((NH, 2, TOKDEV, D), F32),
            pltpu.VMEM((HG, TOK), F32),
            pltpu.VMEM((NZ, NY, HG, TOK), F32),
            dma((6,)),
            dma((NH,)), dma((NH,)),
            dma((2, 4)), dma((2, 15)), dma((2, 17)),
            dma((2, 12)), dma((2, 16)),
            dma((5, NH)), dma((5, NH)),
            dma((NY,)), dma((NY,)), dma((NZ,)), dma((NZ,)),
        ],
        compiler_params=pltpu.CompilerParams(
            collective_id=0, has_side_effects=True, vmem_limit_bytes=48 * 1024 * 1024
        ),
        name="packed_attention",
    )(*(pltpu.with_memory_space_constraint(a, pltpu.HBM) for a in arrays))
    return pl.pallas_call(
        deliver,
        out_shape=shapes,
        in_specs=[pl.BlockSpec(memory_space=pltpu.VMEM)] * 5,
        out_specs=(hbm,) * 5,
        scratch_shapes=[dma((5,))],
        compiler_params=pltpu.CompilerParams(vmem_limit_bytes=2 * 1024 * 1024),
        name="deliver",
    )(*outs)


def solution(mesh):
    return jax.shard_map(
        body,
        mesh=mesh,
        in_specs=(
            P("ctx", "head"), P(("ctx", "head"), None), P(("ctx", "head"), None),
            P("ctx", "head"), P(), P(),
        ),
        out_specs=(
            P("ctx", "head"), P("head", "ctx"), P("ctx", "head"),
            P(("ctx", "head"), None), P(("ctx", "head"), None),
        ),
        check_vma=False,
    )
```
